32 devices in a mesh: groups: 2 (over y), grow: 4 (over z), cross: 2 (over x), side: 2 (over core).
Axes of the slice: x: 2, y: 2, z: 4, core: 2. Of those that a mesh axis runs over, the one named last changes fastest.
Arguments:
- phase_field: float32 [32, 64, 1024], P(('groups', 'grow'), 'cross', 'side'), parts along dimension 0, may hold values from -1.1 to 1.1
- solute_field: float32 [32, 64, 1024], P(('groups', 'grow'), 'cross', 'side'), parts along dimension 0, may hold values from -1 to 0.2
- shift_step: int32 [2], P('groups'), parts along dimension 0, may hold values from 0 to 1
- inflow_seed: int32 [128, 1024], P(('groups', 'cross'), 'side'), parts along dimension 0, may hold values from 0 to 1023
Outputs:
- phase_out: float32 [32, 64, 1024], P(('groups', 'grow'), 'cross', 'side'), parts along dimension 0
- solute_out: float32 [32, 64, 1024], P(('groups', 'grow'), 'cross', 'side'), parts along dimension 0
The draws below stay inside these ranges and needn't reach their ends.
There are 2 independent parts, one for each index of `groups`. The reference program is written for one: setup_inputs(seed, part) draws one part's arguments, and reference() takes and returns one part's arrays. A program takes and returns all parts, laid end to end along the dimension named above; each array names one. Nothing has to cross between parts.
Inputs may be any that keep to these rules, and one draw needn't show every extreme that they name: `shift_step`: the frame moves once, between two of the 3 steps.
All inputs are finite; a program needn't handle non-finite values.
Results may differ from the reference program's by a relative error of at most 0.00002.
Values sent between devices are 32-bit elements; how exact they have to be, the bound alone decides.
A program may use at most 64 MiB of HBM per device.

```python
import jax
import jax.numpy as jnp

ITERS = 3
NZ = 16
NY = 64
NX = 1024


def set_ends(entries, own_key, smallest, largest):
    extent = entries.shape
    place = [jax.random.randint(jax.random.fold_in(own_key, axis), (), 0, extent[axis]) for axis in range(len(extent))]
    entries = entries.at[tuple(place)].set(smallest)
    longest = extent.index(max(extent))
    place[longest] = (place[longest] + 1) % extent[longest]
    return entries.at[tuple(place)].set(largest)


def block_levels(rng, extent, shards, low, high):
    def one(position, shards_of):
        steps = jax.random.uniform(jax.random.fold_in(jax.random.fold_in(rng, 6), position), (shards_of,), jnp.float32, low / len(shards), high / len(shards))
        return jnp.repeat(jnp.exp(steps), extent[position] // shards_of).reshape((-1,) + (1,) * (len(extent) - position - 1))

    loudness = one(*shards[0])
    for cut in shards[1:]:
        loudness = loudness * one(*cut)
    return loudness


def setup_inputs(seed: int = 0, part: int = 0) -> dict:
    key_of = jax.random.split(jax.random.key(seed), 5)
    own_keys = jax.random.split(jax.random.fold_in(key_of[4], part), 5)
    phase_field = jnp.clip(jax.random.uniform(own_keys[0], (NZ, NY, NX), jnp.float32, -1.1, 1.1) * block_levels(own_keys[0], (NZ, NY, NX), ((0, 4), (1, 2), (2, 2)), -0.4, 0.0), -1.1, 1.1)
    solute_field = jnp.clip(-1.0 + 1.2 * jax.random.uniform(own_keys[1], (NZ, NY, NX), jnp.float32) ** block_levels(own_keys[1], (NZ, NY, NX), ((0, 4), (1, 2), (2, 2)), -0.2, 0.2), -1.0, 0.2)
    shift_step = jax.random.randint(own_keys[2], (1,), 0, ITERS - 1).astype(jnp.int32)
    inflow_seed = set_ends(jax.random.randint(own_keys[3], (NY, NX), 0, 1024), jax.random.fold_in(own_keys[3], 1), 0, 1023).astype(jnp.int32)
    return dict(phase_field=phase_field, solute_field=solute_field, shift_step=shift_step, inflow_seed=inflow_seed)


partition = 0.15
coupling = 2.0
diffusion = 2.0
spacing_sq = 0.64
time_step = 0.025
gradient_scale = 1.2
drift_rate = 0.01
seed_levels = 1024.0


def neighbours(side_pad, growth_pad):
    return [growth_pad[:, :-2], growth_pad[:, 2:],
            side_pad[:, :, :-2, 1:-1], side_pad[:, :, 2:, 1:-1],
            side_pad[:, :, 1:-1, :-2], side_pad[:, :, 1:-1, 2:]]


def advance(center, nearby, temper):
    phases = center[0]
    solutes = center[1]
    laplace = -6.0 * phases
    for entry in nearby:
        laplace = laplace + entry[0]
    laplace = laplace / spacing_sq
    slowing = 1.0 - (1.0 - partition) * temper
    driving = laplace + phases - phases * phases * phases - coupling * (1.0 - phases * phases) ** 2 * (solutes + temper)
    growth_rate = driving / slowing
    clipped = jnp.clip(phases, -1.0, 1.0)
    mobile = 0.5 * (1.0 - clipped)
    current = jnp.zeros_like(phases)
    for entry in nearby:
        near_mobile = 0.5 * (1.0 - jnp.clip(entry[0], -1.0, 1.0))
        current = current + 0.5 * (mobile + near_mobile) * (entry[1] - solutes)
    current = current * (diffusion / spacing_sq)
    weight = 0.5 * (1.0 + partition - (1.0 - partition) * clipped)
    solute_rate = (current + 0.5 * (1.0 + (1.0 - partition) * solutes) * growth_rate) / weight
    return jnp.stack([phases + time_step * growth_rate, solutes + time_step * solute_rate])


def reference(phase_field, solute_field, shift_step, inflow_seed):
    planes = phase_field.shape[0]
    frame_step = shift_step[0]
    inflow = inflow_seed.astype(jnp.float32) / seed_levels - 1.0
    top_pair = jnp.stack([jnp.full_like(inflow, -1.0), inflow])[:, None]
    fields = jnp.stack([phase_field, solute_field])
    heights = jnp.arange(planes).astype(jnp.float32)[:, None, None]
    for step_index in range(ITERS):
        window = jnp.pad(fields, ((0, 0), (1, 1), (0, 0), (0, 0)), mode="edge")
        side_pad = jnp.pad(fields, ((0, 0), (0, 0), (1, 1), (1, 1)), mode="wrap")
        nearby = neighbours(side_pad, window)
        shifts = (frame_step < step_index).astype(jnp.float32)
        temper = gradient_scale * ((heights + shifts + 0.5) / planes - 0.5) - drift_rate * step_index
        fields = advance(fields, nearby, temper)
        if step_index < ITERS - 1:
            shifted = jnp.concatenate([fields[:, 1:], top_pair], 1)
            fields = jnp.where(frame_step == step_index, shifted, fields)
    return fields[0], fields[1]
```

```python
import functools

import jax
import jax.numpy as jnp
from jax import lax
from jax.experimental import pallas as pl
from jax.experimental.pallas import tpu as pltpu
from jax.sharding import PartitionSpec as P

partition = 0.15
coupling = 2.0
diffusion = 2.0
spacing_sq = 0.64
time_step = 0.025
gradient_scale = 1.2
drift_rate = 0.01
seed_levels = 1024.0

MESH = pl.DeviceIdType.MESH
EDGE = 4
COL = 128
FIRST = 2


def kernel(sizes, shift_ref, seed_ref, phi_in, sol_in, phi_out, sol_out,
           start, col_next, col_prev, one, two,
           local_sem, z_send, z_recv, y0_send, y0_recv, y_send, y_recv, x_send, x_recv):
    planes, rows, lanes = sizes
    inputs = (phi_in, sol_in)
    gi = lax.axis_index("grow")
    g_last = lax.axis_size("grow") - 1
    ci, c_n = lax.axis_index("cross"), lax.axis_size("cross")
    si, s_n = lax.axis_index("side"), lax.axis_size("side")
    c_next, c_prev = lax.rem(ci + 1, c_n), lax.rem(ci + c_n - 1, c_n)
    s_next, s_prev = lax.rem(si + 1, s_n), lax.rem(si + s_n - 1, s_n)
    at_bottom, at_top = gi == 0, gi == g_last
    inside = (pl.ds(0, rows), pl.ds(0, lanes))

    def remote(src, dst, send, recv, **where):
        return pltpu.make_async_remote_copy(src_ref=src, dst_ref=dst, send_sem=send, recv_sem=recv,
                                            device_id=where, device_id_type=MESH)

    def z_down(field, plane):
        n = 2 * plane + field
        return remote(inputs[field].at[plane], start.at[(field, FIRST + planes + plane) + inside],
                      z_send.at[n], z_recv.at[n], grow=gi - 1)

    def z_up(field, k):
        n = 2 * (planes + k) + field
        return remote(inputs[field].at[planes - 1 - k], start.at[(field, FIRST - 1 - k) + inside],
                      z_send.at[n], z_recv.at[n], grow=gi + 1)

    def y_own(field):
        own = pl.ds(FIRST, planes)
        low = remote(inputs[field].at[:, pl.ds(0, EDGE), :],
                     start.at[field, own, pl.ds(rows, EDGE), pl.ds(0, lanes)],
                     y0_send.at[2 * field], y0_recv.at[2 * field], cross=c_prev)
        high = remote(inputs[field].at[:, pl.ds(rows - EDGE, EDGE), :],
                      start.at[field, own, pl.ds(rows + EDGE, EDGE), pl.ds(0, lanes)],
                      y0_send.at[2 * field + 1], y0_recv.at[2 * field + 1], cross=c_next)
        return low, high

    def y_relay(group, slot):
        low = remote(start.at[:, slot, pl.ds(0, EDGE), pl.ds(0, lanes)],
                     start.at[:, slot, pl.ds(rows, EDGE), pl.ds(0, lanes)],
                     y_send.at[2 * group], y_recv.at[2 * group], cross=c_prev)
        high = remote(start.at[:, slot, pl.ds(rows - EDGE, EDGE), pl.ds(0, lanes)],
                      start.at[:, slot, pl.ds(rows + EDGE, EDGE), pl.ds(0, lanes)],
                      y_send.at[2 * group + 1], y_recv.at[2 * group + 1], cross=c_next)
        return low, high

    def x_copies(group, slot, count):
        own = pl.ds(slot, count)
        low = remote(start.at[:, own, :, pl.ds(0, COL)], col_next.at[:, own],
                     x_send.at[2 * group], x_recv.at[2 * group], side=s_prev)
        high = remote(start.at[:, own, :, pl.ds(lanes - COL, COL)], col_prev.at[:, own],
                      x_send.at[2 * group + 1], x_recv.at[2 * group + 1], side=s_next)
        return low, high

    def combine(slot, count):
        near = lax.broadcasted_iota(jnp.int32, (rows + 2 * EDGE, COL), 1) < COL // 2
        for s in range(slot, slot + count):
            for f in range(2):
                start[f, s, :, pl.ds(lanes, COL)] = jnp.where(near, col_next[f, s], col_prev[f, s])

    wide, tall = lanes + COL, rows + 2 * EDGE
    grid_rows = planes * lax.axis_size("grow")

    def flux(w, u, wn, un):
        return (w + wn) * (un - u)

    def hole(phases):
        return 1.0 - jnp.clip(phases, -1.0, 1.0)

    def advance(center, lower, upper, plane, step):
        p, u = center
        height = (gi * planes + plane).astype(jnp.float32)
        temper = gradient_scale * ((height + 0.5) / grid_rows - 0.5) - drift_rate * step
        w = hole(p)
        total = lower[0] + upper[0]
        flow = flux(w, u, hole(lower[0]), lower[1]) + flux(w, u, hole(upper[0]), upper[1])
        for axis, size in ((0, tall), (1, wide)):
            pn, un = pltpu.roll(p, size - 1, axis), pltpu.roll(u, size - 1, axis)
            total = total + pn + pltpu.roll(p, 1, axis)
            f = flux(w, u, hole(pn), un)
            flow = flow + f - pltpu.roll(f, 1, axis)
        laplace = (total - 6.0 * p) * (1.0 / spacing_sq)
        room = 1.0 - p * p
        driving = laplace + p * room - coupling * (room * room) * (u + temper)
        slowing = 1.0 - (1.0 - partition) * temper
        change = driving * (time_step / jnp.full((1, wide), slowing, jnp.float32))
        gain = flow * (0.5 * time_step * diffusion / spacing_sq) + (1.0 + (1.0 - partition) * u) * change
        weight = 2.0 * partition + (1.0 - partition) * w
        return p + change, u + gain / weight

    def pick(cond, a, b):
        return tuple(jnp.where(cond, x, y) for x, y in zip(a, b))

    def t0(k):
        return start[0, FIRST + k], start[1, FIRST + k]

    def t1(k):
        return one[0, 1 + k], one[1, 1 + k]

    def t2(k):
        return two[0, k], two[1, k]

    def put1(k, v):
        one[0, 1 + k], one[1, 1 + k] = v

    def put2(k, v):
        two[0, k], two[1, k] = v

    moved_early = shift_ref[0] == 0
    last = planes

    def step0(k):
        lower, upper = t0(k - 1), t0(k + 1)
        if k == 0:
            lower = pick(at_bottom, t0(0), lower)
        if k == last - 1:
            upper = pick(at_top, t0(k), upper)
        put1(k, advance(t0(k), lower, upper, k, 0))

    def step1(k):
        put2(k, advance(t1(k), t1(k - 1), t1(k + 1), k, 1))

    def step2(k):
        a, b = advance(t2(k), t2(k - 1), t2(k + 1), k, 2)
        phi_out[k - 1] = a[:rows, :lanes]
        sol_out[k - 1] = b[:rows, :lanes]

    @pl.when(at_top)
    def _():
        start[(0, FIRST + planes) + inside] = jnp.full((rows, lanes), -1.0, jnp.float32)
        start[(1, FIRST + planes) + inside] = seed_ref[...].astype(jnp.float32) / seed_levels - 1.0

    own_copies = [pltpu.make_async_copy(inputs[f], start.at[(f, pl.ds(FIRST, planes)) + inside], local_sem.at[f])
                  for f in range(2)]
    for copy in own_copies:
        copy.start()

    barrier = pltpu.get_barrier_semaphore()
    for where in (dict(cross=c_next), dict(cross=c_prev), dict(side=s_next), dict(side=s_prev)):
        pl.semaphore_signal(barrier, inc=1, device_id=where, device_id_type=MESH)

    @pl.when(jnp.logical_not(at_bottom))
    def _():
        pl.semaphore_signal(barrier, inc=1, device_id=dict(grow=gi - 1), device_id_type=MESH)

    @pl.when(jnp.logical_not(at_top))
    def _():
        pl.semaphore_signal(barrier, inc=1, device_id=dict(grow=gi + 1), device_id_type=MESH)

    ends = at_bottom.astype(jnp.int32) + at_top.astype(jnp.int32)
    pl.semaphore_wait(barrier, 6 - ends)

    fields = range(2)
    has_lower, has_upper = jnp.logical_not(at_bottom), jnp.logical_not(at_top)

    @pl.when(has_lower)
    def _():
        for plane in range(planes):
            for f in fields:
                z_down(f, plane).start()

    @pl.when(has_upper)
    def _():
        for k in range(2):
            for f in fields:
                z_up(f, k).start()

    own_y = [c for f in fields for c in y_own(f)]
    for c in own_y:
        c.start()
    for copy in own_copies:
        copy.wait()
    for c in own_y:
        c.wait_recv()
    own_x = x_copies(0, FIRST, planes)
    for c in own_x:
        c.start()

    below, above = FIRST - 1, FIRST + planes

    def start_y(group, slot):
        for c in y_relay(group, slot):
            c.start()

    def pass_x(group, slot):
        for c in y_relay(group, slot):
            c.wait_recv()
        for c in x_copies(group + 1, slot, 1):
            c.start()

    def finish_x(group, slot):
        for c in x_copies(group + 1, slot, 1):
            c.wait_recv()
        combine(slot, 1)

    for c in own_x:
        c.wait_recv()
    combine(FIRST, planes)
    step0(1)
    step0(2)

    @pl.when(has_lower)
    def _():
        for f in fields:
            z_up(f, 0).wait_recv()
        start_y(0, below)

    @pl.when(has_upper)
    def _():
        for f in fields:
            z_down(f, 0).wait_recv()

    start_y(1, above)

    @pl.when(has_lower)
    def _():
        pass_x(0, below)

    pass_x(1, above)

    @pl.when(has_lower)
    def _():
        finish_x(0, below)

    finish_x(1, above)
    step0(0)
    step0(3)
    put1(0, pick(jnp.logical_and(at_bottom, moved_early), t1(1), t1(0)))
    step1(1)
    step1(2)

    @pl.when(has_upper)
    def _():
        for f in fields:
            z_down(f, 1).wait_recv()
        start_y(2, above + 1)

    @pl.when(has_lower)
    def _():
        for f in fields:
            z_up(f, 1).wait_recv()

    step0(-1)
    put1(-1, pick(at_bottom, t1(0), t1(-1)))
    step1(0)
    put2(0, pick(at_bottom, t2(1), t2(0)))
    step2(1)

    @pl.when(has_upper)
    def _():
        pass_x(2, above + 1)
        finish_x(2, above + 1)

    step0(4)
    put1(4, pick(at_top, pick(moved_early, t0(4), t1(3)), t1(4)))
    step1(3)
    step2(2)

    @pl.when(has_upper)
    def _():
        for f in fields:
            z_down(f, 2).wait_recv()
        start_y(3, above + 2)
        pass_x(3, above + 2)
        finish_x(3, above + 2)

    step0(5)
    put1(5, pick(at_top, t1(4), t1(5)))
    step1(4)
    put2(4, pick(jnp.logical_and(at_top, jnp.logical_not(moved_early)), t0(4), t2(4)))
    step2(3)

    @pl.when(has_upper)
    def _():
        for f in fields:
            z_down(f, 3).wait_recv()

    step0(6)
    step1(5)
    put2(5, pick(at_top, t2(4), t2(5)))
    step2(4)

    for c in own_y + list(own_x):
        c.wait_send()
    for c in y_relay(1, above) + x_copies(2, above, 1):
        c.wait_send()

    @pl.when(has_lower)
    def _():
        for plane in range(planes):
            for f in fields:
                z_down(f, plane).wait_send()
        for c in y_relay(0, below) + x_copies(1, below, 1):
            c.wait_send()

    @pl.when(has_upper)
    def _():
        for k in range(2):
            for f in fields:
                z_up(f, k).wait_send()
        for g in (2, 3):
            for c in y_relay(g, above + g - 1) + x_copies(g + 1, above + g - 1, 1):
                c.wait_send()


def shards(phase_field, solute_field, shift_step, inflow_seed):
    planes, rows, lanes = phase_field.shape
    tall, wide = rows + 2 * EDGE, lanes + COL
    field = jax.ShapeDtypeStruct(phase_field.shape, jnp.float32)
    dma = pltpu.SemaphoreType.DMA
    vmem, hbm = pl.BlockSpec(memory_space=pltpu.VMEM), pl.BlockSpec(memory_space=pl.ANY)
    slots = 2 * planes + 2
    return pl.pallas_call(
        functools.partial(kernel, (planes, rows, lanes)),
        out_shape=(field, field),
        in_specs=[pl.BlockSpec(memory_space=pltpu.SMEM), vmem, hbm, hbm],
        out_specs=(vmem, vmem),
        scratch_shapes=[
            pltpu.VMEM((2, slots, tall, wide), jnp.float32),
            pltpu.VMEM((2, slots, tall, COL), jnp.float32),
            pltpu.VMEM((2, slots, tall, COL), jnp.float32),
            pltpu.VMEM((2, planes + 4, tall, wide), jnp.float32),
            pltpu.VMEM((2, planes + 2, tall, wide), jnp.float32),
            dma((2,)), dma((2 * (planes + 2),)), dma((2 * (planes + 2),)),
            dma((4,)), dma((4,)), dma((8,)), dma((8,)), dma((10,)), dma((10,)),
        ],
        compiler_params=pltpu.CompilerParams(collective_id=0, has_side_effects=True),
    )(shift_step, inflow_seed, phase_field, solute_field)


def solution(mesh):
    return jax.shard_map(
        shards,
        mesh=mesh,
        in_specs=(
            P(("groups", "grow"), "cross", "side"),
            P(("groups", "grow"), "cross", "side"),
            P("groups"),
            P(("groups", "cross"), "side"),
        ),
        out_specs=(P(("groups", "grow"), "cross", "side"), P(("groups", "grow"), "cross", "side")),
        check_vma=False,
    )
```

```python
import functools

import jax
import jax.numpy as jnp
from jax import lax
from jax.experimental import pallas as pl
from jax.experimental.pallas import tpu as pltpu
from jax.sharding import PartitionSpec as P

partition = 0.15
coupling = 2.0
diffusion = 2.0
spacing_sq = 0.64
time_step = 0.025
gradient_scale = 1.2
drift_rate = 0.01
seed_levels = 1024.0

MESH = pl.DeviceIdType.MESH
EDGE = 4
COL = 128
FIRST = 2


def kernel(sizes, shift_ref, seed_ref, phi_in, sol_in, phi_out, sol_out,
           start, col_next, col_prev, one, two, seed_vmem,
           local_sem, diag_send, diag_recv, z_send, z_recv, y0_send, y0_recv, y_send, y_recv, x_send, x_recv):
    planes, rows, lanes = sizes
    inputs = (phi_in, sol_in)
    gi = lax.axis_index("grow")
    g_last = lax.axis_size("grow") - 1
    ci, c_n = lax.axis_index("cross"), lax.axis_size("cross")
    si, s_n = lax.axis_index("side"), lax.axis_size("side")
    c_next, c_prev = lax.rem(ci + 1, c_n), lax.rem(ci + c_n - 1, c_n)
    s_next, s_prev = lax.rem(si + 1, s_n), lax.rem(si + s_n - 1, s_n)
    wide, tall = lanes + COL, rows + 2 * EDGE
    at_bottom, at_top = gi == 0, gi == g_last
    inside = (pl.ds(0, rows), pl.ds(0, lanes))

    def remote(src, dst, send, recv, **where):
        return pltpu.make_async_remote_copy(src_ref=src, dst_ref=dst, send_sem=send, recv_sem=recv,
                                            device_id=where, device_id_type=MESH)

    def z_down(field, plane):
        n = 2 * plane + field
        return remote(inputs[field].at[plane], start.at[(field, FIRST + planes + plane) + inside],
                      z_send.at[n], z_recv.at[n], grow=gi - 1)

    def z_up(field, k):
        n = 2 * (planes + k) + field
        return remote(inputs[field].at[planes - 1 - k], start.at[(field, FIRST - 1 - k) + inside],
                      z_send.at[n], z_recv.at[n], grow=gi + 1)

    def y_pair(src_of, dst_of, count, send, recv, first, **where):
        low = remote(src_of(pl.ds(0, count)), dst_of(pl.ds(rows, count)),
                     send.at[first], recv.at[first], cross=c_prev, **where)
        high = remote(src_of(pl.ds(rows - count, count)), dst_of(pl.ds(tall - count, count)),
                      send.at[first + 1], recv.at[first + 1], cross=c_next, **where)
        return low, high

    def y_own(field):
        return y_pair(lambda r: inputs[field].at[:, r, :],
                      lambda r: start.at[field, pl.ds(FIRST, planes), r, pl.ds(0, lanes)],
                      3, y0_send, y0_recv, 2 * field)

    def y_relay(group, slot):
        view = lambda r: start.at[:, slot, r, pl.ds(0, lanes)]
        return y_pair(view, view, (1, 3, 2)[group], y_send, y_recv, 2 * group)

    def y_diag(field):
        plane = planes - 2
        return y_pair(lambda r: inputs[field].at[plane, r, :],
                      lambda r: start.at[field, FIRST + planes + plane, r, pl.ds(0, lanes)],
                      1, diag_send, diag_recv, 2 * field, grow=gi - 1)

    def x_copies(group, slot, count):
        own = pl.ds(slot, count)
        low = remote(start.at[:, own, :, pl.ds(0, COL)], col_next.at[:, own],
                     x_send.at[2 * group], x_recv.at[2 * group], side=s_prev)
        high = remote(start.at[:, own, :, pl.ds(lanes - COL, COL)], col_prev.at[:, own],
                      x_send.at[2 * group + 1], x_recv.at[2 * group + 1], side=s_next)
        return low, high

    def combine(slot, count):
        near = lax.broadcasted_iota(jnp.int32, (rows + 2 * EDGE, COL), 1) < COL // 2
        for s in range(slot, slot + count):
            for f in range(2):
                start[f, s, :, pl.ds(lanes, COL)] = jnp.where(near, col_next[f, s], col_prev[f, s])

    grid_rows = planes * lax.axis_size("grow")

    def flux(w, u, wn, un):
        return (w + wn) * (un - u)

    def hole(phases):
        return 1.0 - jnp.clip(phases, -1.0, 1.0)

    def advance(center, lower, upper, plane, step):
        p, u = center
        height = (gi * planes + plane).astype(jnp.float32)
        temper = gradient_scale * ((height + 0.5) / grid_rows - 0.5) - drift_rate * step
        w = hole(p)
        total = lower[0] + upper[0]
        flow = flux(w, u, hole(lower[0]), lower[1]) + flux(w, u, hole(upper[0]), upper[1])
        for axis, size in ((0, tall), (1, wide)):
            pn, un = pltpu.roll(p, size - 1, axis), pltpu.roll(u, size - 1, axis)
            total = total + pn + pltpu.roll(p, 1, axis)
            f = flux(w, u, hole(pn), un)
            flow = flow + f - pltpu.roll(f, 1, axis)
        laplace = (total - 6.0 * p) * (1.0 / spacing_sq)
        room = 1.0 - p * p
        driving = laplace + p * room - coupling * (room * room) * (u + temper)
        slowing = 1.0 - (1.0 - partition) * temper
        change = driving * (time_step / jnp.full((1, wide), slowing, jnp.float32))
        gain = flow * (0.5 * time_step * diffusion / spacing_sq) + (1.0 + (1.0 - partition) * u) * change
        weight = 2.0 * partition + (1.0 - partition) * w
        return p + change, u + gain / weight

    def pick(cond, a, b):
        return tuple(jnp.where(cond, x, y) for x, y in zip(a, b))

    def t0(k):
        return start[0, FIRST + k], start[1, FIRST + k]

    def t1(k):
        return one[0, 1 + k], one[1, 1 + k]

    def t2(k):
        return two[0, k], two[1, k]

    def put1(k, v):
        one[0, 1 + k], one[1, 1 + k] = v

    def put2(k, v):
        two[0, k], two[1, k] = v

    last = planes

    def step0(k):
        lower, upper = t0(k - 1), t0(k + 1)
        if k == 0:
            lower = pick(at_bottom, t0(0), lower)
        if k == last - 1:
            upper = pick(at_top, t0(k), upper)
        put1(k, advance(t0(k), lower, upper, k, 0))

    def step1(k):
        put2(k, advance(t1(k), t1(k - 1), t1(k + 1), k, 1))

    def step2(k):
        a, b = advance(t2(k), t2(k - 1), t2(k + 1), k, 2)
        phi_out[k - 1] = a[:rows, :lanes]
        sol_out[k - 1] = b[:rows, :lanes]

    own_copies = [pltpu.make_async_copy(inputs[f], start.at[(f, pl.ds(FIRST, planes)) + inside], local_sem.at[f])
                  for f in range(2)]
    for copy in own_copies:
        copy.start()

    @pl.when(at_top)
    def _():
        seeds = pltpu.make_async_copy(seed_ref, seed_vmem, local_sem.at[2])
        seeds.start()
        seeds.wait()
        start[(0, FIRST + planes) + inside] = jnp.full((rows, lanes), -1.0, jnp.float32)
        start[(1, FIRST + planes) + inside] = seed_vmem[...].astype(jnp.float32) / seed_levels - 1.0

    barrier = pltpu.get_barrier_semaphore()
    for where in (dict(cross=c_next), dict(cross=c_prev), dict(side=s_next), dict(side=s_prev)):
        pl.semaphore_signal(barrier, inc=1, device_id=where, device_id_type=MESH)

    for edge, near in ((at_bottom, gi - 1), (at_top, gi + 1)):
        @pl.when(jnp.logical_not(edge))
        def _():
            for where in (dict(grow=near), dict(grow=near, cross=c_next), dict(grow=near, cross=c_prev)):
                pl.semaphore_signal(barrier, inc=1, device_id=where, device_id_type=MESH)

    ends = at_bottom.astype(jnp.int32) + at_top.astype(jnp.int32)
    pl.semaphore_wait(barrier, 10 - 3 * ends)

    fields = range(2)
    has_lower, has_upper = jnp.logical_not(at_bottom), jnp.logical_not(at_top)

    @pl.when(has_lower)
    def _():
        for plane in range(planes):
            for f in fields:
                z_down(f, plane).start()
            if plane == 0:
                for f in fields:
                    for c in y_diag(f):
                        c.start()

    @pl.when(has_upper)
    def _():
        for k in range(2):
            for f in fields:
                z_up(f, k).start()

    own_y = [c for f in fields for c in y_own(f)]
    for c in own_y:
        c.start()
    for copy in own_copies:
        copy.wait()
    for c in own_y:
        c.wait_recv()
    own_x = x_copies(0, FIRST, planes)
    for c in own_x:
        c.start()

    below, above = FIRST - 1, FIRST + planes

    def start_y(group, slot):
        for c in y_relay(group, slot):
            c.start()

    def pass_x(group, slot):
        for c in y_relay(group, slot):
            c.wait_recv()
        for c in x_copies(group + 1, slot, 1):
            c.start()

    def finish_x(group, slot):
        for c in x_copies(group + 1, slot, 1):
            c.wait_recv()
        combine(slot, 1)

    moved_early = shift_ref[0] == 0

    @pl.when(has_lower)
    def _():
        for f in fields:
            z_up(f, 0).wait_recv()
        start_y(0, below)

    @pl.when(has_upper)
    def _():
        for f in fields:
            z_down(f, 0).wait_recv()

    start_y(1, above)
    for c in own_x:
        c.wait_recv()
    combine(FIRST, planes)
    step0(1)
    step0(2)

    @pl.when(has_lower)
    def _():
        pass_x(0, below)

    pass_x(1, above)

    @pl.when(has_upper)
    def _():
        for f in fields:
            z_down(f, 1).wait_recv()
        start_y(2, above + 1)

    @pl.when(has_lower)
    def _():
        finish_x(0, below)

    finish_x(1, above)
    step0(0)
    step0(3)
    put1(0, pick(jnp.logical_and(at_bottom, moved_early), t1(1), t1(0)))
    step1(1)
    step1(2)

    @pl.when(has_lower)
    def _():
        for f in fields:
            z_up(f, 1).wait_recv()

    step0(-1)
    put1(-1, pick(at_bottom, t1(0), t1(-1)))
    step1(0)
    put2(0, pick(at_bottom, t2(1), t2(0)))
    step2(1)

    @pl.when(has_upper)
    def _():
        pass_x(2, above + 1)
        for f in fields:
            z_down(f, 2).wait_recv()
            for c in y_diag(f):
                c.wait_recv()
        for c in x_copies(4, above + 2, 1):
            c.start()
        finish_x(2, above + 1)

    step0(4)
    put1(4, pick(at_top, pick(moved_early, t0(4), t1(3)), t1(4)))
    step1(3)
    step2(2)

    @pl.when(has_upper)
    def _():
        finish_x(3, above + 2)

    step0(5)
    put1(5, pick(at_top, t1(4), t1(5)))
    step1(4)
    put2(4, pick(jnp.logical_and(at_top, jnp.logical_not(moved_early)), t0(4), t2(4)))
    step2(3)

    @pl.when(has_upper)
    def _():
        for f in fields:
            z_down(f, 3).wait_recv()

    step0(6)
    step1(5)
    put2(5, pick(at_top, t2(4), t2(5)))
    step2(4)

    for c in own_y + list(own_x):
        c.wait_send()
    for c in y_relay(1, above) + x_copies(2, above, 1):
        c.wait_send()

    @pl.when(has_lower)
    def _():
        for plane in range(planes):
            for f in fields:
                z_down(f, plane).wait_send()
        for f in fields:
            for c in y_diag(f):
                c.wait_send()
        for c in y_relay(0, below) + x_copies(1, below, 1):
            c.wait_send()

    @pl.when(has_upper)
    def _():
        for k in range(2):
            for f in fields:
                z_up(f, k).wait_send()
        for c in y_relay(2, above + 1) + x_copies(3, above + 1, 1) + x_copies(4, above + 2, 1):
            c.wait_send()


def shards(phase_field, solute_field, shift_step, inflow_seed):
    planes, rows, lanes = phase_field.shape
    tall, wide = rows + 2 * EDGE, lanes + COL
    field = jax.ShapeDtypeStruct(phase_field.shape, jnp.float32)
    dma = pltpu.SemaphoreType.DMA
    vmem, hbm = pl.BlockSpec(memory_space=pltpu.VMEM), pl.BlockSpec(memory_space=pl.ANY)
    slots = 2 * planes + 2
    on_chip = pltpu.VMEM(phase_field.shape, jnp.float32)
    return pl.pallas_call(
        functools.partial(kernel, (planes, rows, lanes)),
        out_shape=(on_chip, on_chip),
        in_specs=[pl.BlockSpec(memory_space=pltpu.SMEM), hbm, hbm, hbm],
        out_specs=(vmem, vmem),
        scratch_shapes=[
            pltpu.VMEM((2, slots, tall, wide), jnp.float32),
            pltpu.VMEM((2, slots, tall, COL), jnp.float32),
            pltpu.VMEM((2, slots, tall, COL), jnp.float32),
            pltpu.VMEM((2, planes + 4, tall, wide), jnp.float32),
            pltpu.VMEM((2, planes + 2, tall, wide), jnp.float32),
            pltpu.VMEM((rows, lanes), jnp.int32),
            dma((3,)), dma((4,)), dma((4,)), dma((2 * (planes + 2),)), dma((2 * (planes + 2),)),
            dma((4,)), dma((4,)), dma((6,)), dma((6,)), dma((10,)), dma((10,)),
        ],
        compiler_params=pltpu.CompilerParams(collective_id=0, has_side_effects=True),
    )(shift_step, inflow_seed, phase_field, solute_field)


def solution(mesh):
    return jax.shard_map(
        shards,
        mesh=mesh,
        in_specs=(
            P(("groups", "grow"), "cross", "side"),
            P(("groups", "grow"), "cross", "side"),
            P("groups"),
            P(("groups", "cross"), "side"),
        ),
        out_specs=(P(("groups", "grow"), "cross", "side"), P(("groups", "grow"), "cross", "side")),
        check_vma=False,
    )
```

```python
import functools

import jax
import jax.numpy as jnp
from jax import lax
from jax.experimental import pallas as pl
from jax.experimental.pallas import tpu as pltpu
from jax.sharding import PartitionSpec as P

partition = 0.15
coupling = 2.0
diffusion = 2.0
spacing_sq = 0.64
time_step = 0.025
gradient_scale = 1.2
drift_rate = 0.01
seed_levels = 1024.0

MESH = pl.DeviceIdType.MESH
EDGE = 4
COL = 128
FIRST = 2


def kernel(sizes, shift_ref, seed_ref, phi_in, sol_in, phi_out, sol_out,
           start, col_next, col_prev, one, two, seed_vmem,
           local_sem, diag_send, diag_recv, z_send, z_recv, y0_send, y0_recv, y_send, y_recv, x_send, x_recv):
    planes, rows, lanes = sizes
    inputs = (phi_in, sol_in)
    gi = lax.axis_index("grow")
    g_last = lax.axis_size("grow") - 1
    ci, c_n = lax.axis_index("cross"), lax.axis_size("cross")
    si, s_n = lax.axis_index("side"), lax.axis_size("side")
    c_next, c_prev = lax.rem(ci + 1, c_n), lax.rem(ci + c_n - 1, c_n)
    s_next, s_prev = lax.rem(si + 1, s_n), lax.rem(si + s_n - 1, s_n)
    wide, tall = lanes + COL, rows + 2 * EDGE
    at_bottom, at_top = gi == 0, gi == g_last
    inside = (pl.ds(0, rows), pl.ds(0, lanes))

    def remote(src, dst, send, recv, **where):
        return pltpu.make_async_remote_copy(src_ref=src, dst_ref=dst, send_sem=send, recv_sem=recv,
                                            device_id=where, device_id_type=MESH)

    def z_down(field, plane):
        n = 2 * plane + field
        return remote(inputs[field].at[plane], start.at[(field, FIRST + planes + plane) + inside],
                      z_send.at[n], z_recv.at[n], grow=gi - 1)

    def z_up(field, k):
        n = 2 * (planes + k) + field
        return remote(inputs[field].at[planes - 1 - k], start.at[(field, FIRST - 1 - k) + inside],
                      z_send.at[n], z_recv.at[n], grow=gi + 1)

    def y_pair(src_of, dst_of, count, send, recv, first, **where):
        low = remote(src_of(pl.ds(0, count)), dst_of(pl.ds(rows, count)),
                     send.at[first], recv.at[first], cross=c_prev, **where)
        high = remote(src_of(pl.ds(rows - count, count)), dst_of(pl.ds(tall - count, count)),
                      send.at[first + 1], recv.at[first + 1], cross=c_next, **where)
        return low, high

    def y_own(field):
        return y_pair(lambda r: inputs[field].at[:, r, :],
                      lambda r: start.at[field, pl.ds(FIRST, planes), r, pl.ds(0, lanes)],
                      3, y0_send, y0_recv, 2 * field)

    def y_relay(group, slot):
        view = lambda r: start.at[:, slot, r, pl.ds(0, lanes)]
        return y_pair(view, view, (1, 3, 2)[group], y_send, y_recv, 2 * group)

    def y_diag(field):
        plane = planes - 2
        return y_pair(lambda r: inputs[field].at[plane, r, :],
                      lambda r: start.at[field, FIRST + planes + plane, r, pl.ds(0, lanes)],
                      1, diag_send, diag_recv, 2 * field, grow=gi - 1)

    def x_copies(group, slot, count):
        own = pl.ds(slot, count)
        low = remote(start.at[:, own, :, pl.ds(0, COL)], col_next.at[:, own],
                     x_send.at[2 * group], x_recv.at[2 * group], side=s_prev)
        high = remote(start.at[:, own, :, pl.ds(lanes - COL, COL)], col_prev.at[:, own],
                      x_send.at[2 * group + 1], x_recv.at[2 * group + 1], side=s_next)
        return low, high

    def combine(slot, count):
        near = lax.broadcasted_iota(jnp.int32, (rows + 2 * EDGE, COL), 1) < COL // 2
        for s in range(slot, slot + count):
            for f in range(2):
                start[f, s, :, pl.ds(lanes, COL)] = jnp.where(near, col_next[f, s], col_prev[f, s])

    grid_rows = planes * lax.axis_size("grow")

    def flux(w, u, wn, un):
        return (w + wn) * (un - u)

    def hole(phases):
        return 1.0 - jnp.clip(phases, -1.0, 1.0)

    def advance(center, lower, upper, plane, step):
        p, u = center
        height = (gi * planes + plane).astype(jnp.float32)
        temper = gradient_scale * ((height + 0.5) / grid_rows - 0.5) - drift_rate * step
        w = hole(p)
        total = lower[0] + upper[0]
        flow = flux(w, u, hole(lower[0]), lower[1]) + flux(w, u, hole(upper[0]), upper[1])
        for axis, size in ((0, tall), (1, wide)):
            pn, un = pltpu.roll(p, size - 1, axis), pltpu.roll(u, size - 1, axis)
            total = total + pn + pltpu.roll(p, 1, axis)
            f = flux(w, u, hole(pn), un)
            flow = flow + f - pltpu.roll(f, 1, axis)
        laplace = (total - 6.0 * p) * (1.0 / spacing_sq)
        room = 1.0 - p * p
        driving = laplace + p * room - coupling * (room * room) * (u + temper)
        slowing = 1.0 - (1.0 - partition) * temper
        change = driving * (time_step / jnp.full((1, wide), slowing, jnp.float32))
        gain = flow * (0.5 * time_step * diffusion / spacing_sq) + (1.0 + (1.0 - partition) * u) * change
        weight = 2.0 * partition + (1.0 - partition) * w
        return p + change, u + gain / weight

    def pick(cond, a, b):
        return tuple(jnp.where(cond, x, y) for x, y in zip(a, b))

    def t0(k):
        return start[0, FIRST + k], start[1, FIRST + k]

    def t1(k):
        return one[0, 1 + k], one[1, 1 + k]

    def t2(k):
        return two[0, k], two[1, k]

    def put1(k, v):
        one[0, 1 + k], one[1, 1 + k] = v

    def put2(k, v):
        two[0, k], two[1, k] = v

    last = planes

    def step0(k):
        lower, upper = t0(k - 1), t0(k + 1)
        if k == 0:
            lower = pick(at_bottom, t0(0), lower)
        if k == last - 1:
            upper = pick(at_top, t0(k), upper)
        put1(k, advance(t0(k), lower, upper, k, 0))

    def step1(k):
        put2(k, advance(t1(k), t1(k - 1), t1(k + 1), k, 1))

    def step2(k):
        a, b = advance(t2(k), t2(k - 1), t2(k + 1), k, 2)
        phi_out[k - 1] = a[:rows, :lanes]
        sol_out[k - 1] = b[:rows, :lanes]

    own_copies = [pltpu.make_async_copy(inputs[f], start.at[(f, pl.ds(FIRST, planes)) + inside], local_sem.at[f])
                  for f in range(2)]
    for copy in own_copies:
        copy.start()

    @pl.when(at_top)
    def _():
        seeds = pltpu.make_async_copy(seed_ref, seed_vmem, local_sem.at[2])
        seeds.start()
        seeds.wait()
        start[(0, FIRST + planes) + inside] = jnp.full((rows, lanes), -1.0, jnp.float32)
        start[(1, FIRST + planes) + inside] = seed_vmem[...].astype(jnp.float32) / seed_levels - 1.0

    barrier = pltpu.get_barrier_semaphore()
    for where in (dict(cross=c_next), dict(cross=c_prev), dict(side=s_next), dict(side=s_prev)):
        pl.semaphore_signal(barrier, inc=1, device_id=where, device_id_type=MESH)

    for edge, near in ((at_bottom, gi - 1), (at_top, gi + 1)):
        @pl.when(jnp.logical_not(edge))
        def _():
            for where in (dict(grow=near), dict(grow=near, cross=c_next), dict(grow=near, cross=c_prev)):
                pl.semaphore_signal(barrier, inc=1, device_id=where, device_id_type=MESH)

    ends = at_bottom.astype(jnp.int32) + at_top.astype(jnp.int32)
    pl.semaphore_wait(barrier, 10 - 3 * ends)

    fields = range(2)
    has_lower, has_upper = jnp.logical_not(at_bottom), jnp.logical_not(at_top)

    @pl.when(has_lower)
    def _():
        for plane in range(planes):
            for f in fields:
                z_down(f, plane).start()
            if plane == 0:
                for f in fields:
                    for c in y_diag(f):
                        c.start()

    @pl.when(has_upper)
    def _():
        for k in range(2):
            for f in fields:
                z_up(f, k).start()

    own_y = [c for f in fields for c in y_own(f)]
    for c in own_y:
        c.start()
    for copy in own_copies:
        copy.wait()
    for c in own_y:
        c.wait_recv()
    own_x = x_copies(0, FIRST, planes)
    for c in own_x:
        c.start()

    below, above = FIRST - 1, FIRST + planes

    def start_y(group, slot):
        for c in y_relay(group, slot):
            c.start()

    def pass_x(group, slot):
        for c in y_relay(group, slot):
            c.wait_recv()
        for c in x_copies(group + 1, slot, 1):
            c.start()

    def finish_x(group, slot):
        for c in x_copies(group + 1, slot, 1):
            c.wait_recv()
        combine(slot, 1)

    moved_early = shift_ref[0] == 0

    @pl.when(has_lower)
    def _():
        for f in fields:
            z_up(f, 0).wait_recv()
        start_y(0, below)

    @pl.when(has_upper)
    def _():
        for f in fields:
            z_down(f, 0).wait_recv()

    start_y(1, above)
    for c in own_x:
        c.wait_recv()
    combine(FIRST, planes)
    step0(1)
    step0(2)

    @pl.when(has_lower)
    def _():
        pass_x(0, below)

    pass_x(1, above)

    @pl.when(has_upper)
    def _():
        for f in fields:
            z_down(f, 1).wait_recv()
        start_y(2, above + 1)

    @pl.when(has_lower)
    def _():
        finish_x(0, below)

    finish_x(1, above)
    step0(0)
    step0(3)
    put1(0, pick(jnp.logical_and(at_bottom, moved_early), t1(1), t1(0)))
    step1(1)
    step1(2)

    @pl.when(has_lower)
    def _():
        for f in fields:
            z_up(f, 1).wait_recv()

    step0(-1)
    put1(-1, pick(at_bottom, t1(0), t1(-1)))
    step1(0)
    put2(0, pick(at_bottom, t2(1), t2(0)))
    step2(1)

    @pl.when(has_upper)
    def _():
        pass_x(2, above + 1)
        for f in fields:
            z_down(f, 2).wait_recv()
            for c in y_diag(f):
                c.wait_recv()
        for c in x_copies(4, above + 2, 1):
            c.start()
        finish_x(2, above + 1)

    step0(4)
    put1(4, pick(at_top, pick(moved_early, t0(4), t1(3)), t1(4)))
    step1(3)
    step2(2)

    @pl.when(has_upper)
    def _():
        finish_x(3, above + 2)

    step0(5)
    put1(5, pick(at_top, t1(4), t1(5)))
    step1(4)
    put2(4, pick(jnp.logical_and(at_top, jnp.logical_not(moved_early)), t0(4), t2(4)))
    step2(3)

    @pl.when(has_upper)
    def _():
        for f in fields:
            z_down(f, 3).wait_recv()

    step0(6)
    step1(5)
    put2(5, pick(at_top, t2(4), t2(5)))
    step2(4)

    for c in own_y + list(own_x):
        c.wait_send()
    for c in y_relay(1, above) + x_copies(2, above, 1):
        c.wait_send()

    @pl.when(has_lower)
    def _():
        for plane in range(planes):
            for f in fields:
                z_down(f, plane).wait_send()
        for f in fields:
            for c in y_diag(f):
                c.wait_send()
        for c in y_relay(0, below) + x_copies(1, below, 1):
            c.wait_send()

    @pl.when(has_upper)
    def _():
        for k in range(2):
            for f in fields:
                z_up(f, k).wait_send()
        for c in y_relay(2, above + 1) + x_copies(3, above + 1, 1) + x_copies(4, above + 2, 1):
            c.wait_send()


def write_out(phi_ref, sol_ref, phi_out, sol_out, sem):
    copies = [pltpu.make_async_copy(phi_ref, phi_out, sem.at[0]), pltpu.make_async_copy(sol_ref, sol_out, sem.at[1])]
    for copy in copies:
        copy.start()
    for copy in copies:
        copy.wait()


def shards(phase_field, solute_field, shift_step, inflow_seed):
    planes, rows, lanes = phase_field.shape
    tall, wide = rows + 2 * EDGE, lanes + COL
    field = jax.ShapeDtypeStruct(phase_field.shape, jnp.float32)
    dma = pltpu.SemaphoreType.DMA
    vmem, hbm = pl.BlockSpec(memory_space=pltpu.VMEM), pl.BlockSpec(memory_space=pl.ANY)
    slots = 2 * planes + 2
    on_chip = pltpu.VMEM(phase_field.shape, jnp.float32)
    results = pl.pallas_call(
        functools.partial(kernel, (planes, rows, lanes)),
        out_shape=(on_chip, on_chip),
        in_specs=[pl.BlockSpec(memory_space=pltpu.SMEM), hbm, hbm, hbm],
        out_specs=(vmem, vmem),
        scratch_shapes=[
            pltpu.VMEM((2, slots, tall, wide), jnp.float32),
            pltpu.VMEM((2, slots, tall, COL), jnp.float32),
            pltpu.VMEM((2, slots, tall, COL), jnp.float32),
            pltpu.VMEM((2, planes + 4, tall, wide), jnp.float32),
            pltpu.VMEM((2, planes + 2, tall, wide), jnp.float32),
            pltpu.VMEM((rows, lanes), jnp.int32),
            dma((3,)), dma((4,)), dma((4,)), dma((2 * (planes + 2),)), dma((2 * (planes + 2),)),
            dma((4,)), dma((4,)), dma((6,)), dma((6,)), dma((10,)), dma((10,)),
        ],
        compiler_params=pltpu.CompilerParams(collective_id=0, has_side_effects=True),
    )(shift_step, inflow_seed, phase_field, solute_field)
    return pl.pallas_call(
        write_out,
        out_shape=(field, field),
        in_specs=[vmem, vmem],
        out_specs=(hbm, hbm),
        scratch_shapes=[dma((2,))],
    )(*(pltpu.with_memory_space_constraint(x, pltpu.VMEM) for x in results))


def solution(mesh):
    return jax.shard_map(
        shards,
        mesh=mesh,
        in_specs=(
            P(("groups", "grow"), "cross", "side"),
            P(("groups", "grow"), "cross", "side"),
            P("groups"),
            P(("groups", "cross"), "side"),
        ),
        out_specs=(P(("groups", "grow"), "cross", "side"), P(("groups", "grow"), "cross", "side")),
        check_vma=False,
    )
```

```python
import functools

import jax
import jax.numpy as jnp
from jax import lax
from jax.experimental import pallas as pl
from jax.experimental.pallas import tpu as pltpu
from jax.sharding import PartitionSpec as P

partition = 0.15
coupling = 2.0
diffusion = 2.0
spacing_sq = 0.64
time_step = 0.025
gradient_scale = 1.2
drift_rate = 0.01
seed_levels = 1024.0

MESH = pl.DeviceIdType.MESH
EDGE = 4
TILE = 8
COL = 128
FIRST = 2


def kernel(sizes, shift_ref, seed_ref, phi_in, sol_in, phi_out, sol_out,
           start, col_next, col_prev, one, two, edges, seed_vmem,
           local_sem, edge_send, edge_recv, last_send, last_recv, z_send, z_recv, y0_send, y0_recv, y_send, y_recv, x_send, x_recv):
    planes, rows, lanes = sizes
    inputs = (phi_in, sol_in)
    gi = lax.axis_index("grow")
    g_last = lax.axis_size("grow") - 1
    ci, c_n = lax.axis_index("cross"), lax.axis_size("cross")
    si, s_n = lax.axis_index("side"), lax.axis_size("side")
    c_next, c_prev = lax.rem(ci + 1, c_n), lax.rem(ci + c_n - 1, c_n)
    s_next, s_prev = lax.rem(si + 1, s_n), lax.rem(si + s_n - 1, s_n)
    wide, tall = lanes + COL, rows + 2 * EDGE
    at_bottom, at_top = gi == 0, gi == g_last
    inside = (pl.ds(0, rows), pl.ds(0, lanes))

    def remote(src, dst, send, recv, **where):
        return pltpu.make_async_remote_copy(src_ref=src, dst_ref=dst, send_sem=send, recv_sem=recv,
                                            device_id=where, device_id_type=MESH)

    def z_down(field, plane):
        n = 2 * plane + field
        return remote(inputs[field].at[plane], start.at[(field, FIRST + planes + plane) + inside],
                      z_send.at[n], z_recv.at[n], grow=gi - 1)

    def z_up(field, k):
        n = 2 * (planes + k) + field
        return remote(inputs[field].at[planes - 1 - k], start.at[(field, FIRST - 1 - k) + inside],
                      z_send.at[n], z_recv.at[n], grow=gi + 1)

    def y_pair(src_of, dst_of, count, send, recv, first, **where):
        low = remote(src_of(pl.ds(0, count)), dst_of(pl.ds(rows, count)),
                     send.at[first], recv.at[first], cross=c_prev, **where)
        high = remote(src_of(pl.ds(rows - count, count)), dst_of(pl.ds(tall - count, count)),
                      send.at[first + 1], recv.at[first + 1], cross=c_next, **where)
        return low, high

    def y_own(field):
        return y_pair(lambda r: inputs[field].at[:, r, :],
                      lambda r: start.at[field, pl.ds(FIRST, planes), r, pl.ds(0, lanes)],
                      3, y0_send, y0_recv, 2 * field)

    def y_relay(group, slot):
        view = lambda r: start.at[:, slot, r, pl.ds(0, lanes)]
        return y_pair(view, view, (1, 3, 2)[group], y_send, y_recv, 2 * group)

    def z_edge(field):
        plane = inputs[field].at[planes - 2]
        return [remote(plane.at[pl.ds(row, 1), :], edges.at[field, side, pl.ds(0, 1), :],
                       edge_send.at[2 * field + side], edge_recv.at[2 * field + side], grow=gi - 1)
                for side, row in ((0, 0), (1, rows - 1))]

    def y_edge(side):
        row, where = ((rows, c_prev), (tall - 1, c_next))[side]
        return remote(edges.at[:, side, pl.ds(0, 1), :],
                      start.at[:, FIRST + 2 * planes - 2, pl.ds(row, 1), pl.ds(0, lanes)],
                      edge_send.at[4 + side], edge_recv.at[4 + side], cross=where)

    def z_last(field, r):
        part = pl.ds(TILE * r, TILE)
        return remote(inputs[field].at[planes - 1, part, :],
                      start.at[field, FIRST + 2 * planes - 1, part, pl.ds(0, lanes)],
                      last_send.at[2 * r + field], last_recv.at[2 * r + field], grow=gi - 1)

    def x_copies(group, slot, count):
        own = pl.ds(slot, count)
        low = remote(start.at[:, own, :, pl.ds(0, COL)], col_next.at[:, own],
                     x_send.at[2 * group], x_recv.at[2 * group], side=s_prev)
        high = remote(start.at[:, own, :, pl.ds(lanes - COL, COL)], col_prev.at[:, own],
                      x_send.at[2 * group + 1], x_recv.at[2 * group + 1], side=s_next)
        return low, high

    def combine(slot, count):
        near = lax.broadcasted_iota(jnp.int32, (rows + 2 * EDGE, COL), 1) < COL // 2
        for s in range(slot, slot + count):
            for f in range(2):
                start[f, s, :, pl.ds(lanes, COL)] = jnp.where(near, col_next[f, s], col_prev[f, s])

    grid_rows = planes * lax.axis_size("grow")

    def flux(w, u, wn, un):
        return (w + wn) * (un - u)

    def hole(phases):
        return 1.0 - jnp.clip(phases, -1.0, 1.0)

    def update(p, u, w, total, flow, plane, step):
        height = (gi * planes + plane).astype(jnp.float32)
        temper = gradient_scale * ((height + 0.5) / grid_rows - 0.5) - drift_rate * step
        laplace = (total - 6.0 * p) * (1.0 / spacing_sq)
        room = 1.0 - p * p
        driving = laplace + p * room - coupling * (room * room) * (u + temper)
        slowing = 1.0 - (1.0 - partition) * temper
        change = driving * (time_step / jnp.full((1, wide), slowing, jnp.float32))
        gain = flow * (0.5 * time_step * diffusion / spacing_sq) + (1.0 + (1.0 - partition) * u) * change
        weight = 2.0 * partition + (1.0 - partition) * w
        return p + change, u + gain / weight

    def along(p, u, w, axis, size):
        pn, un = pltpu.roll(p, size - 1, axis), pltpu.roll(u, size - 1, axis)
        f = flux(w, u, hole(pn), un)
        return pn + pltpu.roll(p, 1, axis), f - pltpu.roll(f, 1, axis)

    def advance(center, lower, upper, plane, step):
        p, u = center
        w = hole(p)
        total = lower[0] + upper[0]
        flow = flux(w, u, hole(lower[0]), lower[1]) + flux(w, u, hole(upper[0]), upper[1])
        for axis, size in ((0, tall), (1, wide)):
            t, f = along(p, u, w, axis, size)
            total, flow = total + t, flow + f
        return update(p, u, w, total, flow, plane, step)

    def tile(buf, slot, r):
        part = pl.ds(TILE * r, TILE)
        return buf[0, slot, part, :], buf[1, slot, part, :]

    def advance_tile(buf, slot, r, lower, upper, plane, step):
        count = tall // TILE
        p, u = tile(buf, slot, r)
        before, after = tile(buf, slot, (r - 1) % count), tile(buf, slot, (r + 1) % count)
        w = hole(p)
        total, flow = along(p, u, w, 1, wide)
        pb, ub = (pltpu.roll(jnp.concatenate([a, b]), 1, 0)[TILE:] for a, b in zip(before, (p, u)))
        pa, ua = (pltpu.roll(jnp.concatenate([b, a]), 2 * TILE - 1, 0)[:TILE] for a, b in zip(after, (p, u)))
        for pn, un in ((pb, ub), (pa, ua), lower, upper):
            total, flow = total + pn, flow + flux(w, u, hole(pn), un)
        return update(p, u, w, total, flow, plane, step)

    def pick(cond, a, b):
        return tuple(jnp.where(cond, x, y) for x, y in zip(a, b))

    def t0(k):
        return start[0, FIRST + k], start[1, FIRST + k]

    def t1(k):
        return one[0, 1 + k], one[1, 1 + k]

    def t2(k):
        return two[0, k], two[1, k]

    def put1(k, v):
        one[0, 1 + k], one[1, 1 + k] = v

    def put2(k, v):
        two[0, k], two[1, k] = v

    last = planes

    def step0(k):
        lower, upper = t0(k - 1), t0(k + 1)
        if k == 0:
            lower = pick(at_bottom, t0(0), lower)
        if k == last - 1:
            upper = pick(at_top, t0(k), upper)
        put1(k, advance(t0(k), lower, upper, k, 0))

    def step1(k):
        put2(k, advance(t1(k), t1(k - 1), t1(k + 1), k, 1))

    def step2(k):
        a, b = advance(t2(k), t2(k - 1), t2(k + 1), k, 2)
        phi_out[k - 1] = a[:rows, :lanes]
        sol_out[k - 1] = b[:rows, :lanes]

    own_copies = [pltpu.make_async_copy(inputs[f], start.at[(f, pl.ds(FIRST, planes)) + inside], local_sem.at[f])
                  for f in range(2)]
    for copy in own_copies:
        copy.start()

    @pl.when(at_top)
    def _():
        seeds = pltpu.make_async_copy(seed_ref, seed_vmem, local_sem.at[2])
        seeds.start()
        seeds.wait()
        start[(0, FIRST + planes) + inside] = jnp.full((rows, lanes), -1.0, jnp.float32)
        start[(1, FIRST + planes) + inside] = seed_vmem[...].astype(jnp.float32) / seed_levels - 1.0

    barrier = pltpu.get_barrier_semaphore()
    for where in (dict(cross=c_next), dict(cross=c_prev), dict(side=s_next), dict(side=s_prev)):
        pl.semaphore_signal(barrier, inc=1, device_id=where, device_id_type=MESH)

    for edge, near in ((at_bottom, gi - 1), (at_top, gi + 1)):
        @pl.when(jnp.logical_not(edge))
        def _():
            pl.semaphore_signal(barrier, inc=1, device_id=dict(grow=near), device_id_type=MESH)

    ends = at_bottom.astype(jnp.int32) + at_top.astype(jnp.int32)
    pl.semaphore_wait(barrier, 6 - ends)

    fields = range(2)
    has_lower, has_upper = jnp.logical_not(at_bottom), jnp.logical_not(at_top)

    @pl.when(has_lower)
    def _():
        for plane in range(planes - 1):
            for f in fields:
                z_down(f, plane).start()
            if plane == 0:
                for f in fields:
                    for c in z_edge(f):
                        c.start()
        for r in range(rows // TILE):
            for f in fields:
                z_last(f, r).start()

    @pl.when(has_upper)
    def _():
        for k in range(2):
            for f in fields:
                z_up(f, k).start()

    own_y = [c for f in fields for c in y_own(f)]
    for c in own_y:
        c.start()
    for copy in own_copies:
        copy.wait()
    for c in own_y:
        c.wait_recv()
    own_x = x_copies(0, FIRST, planes)
    for c in own_x:
        c.start()

    below, above = FIRST - 1, FIRST + planes

    def start_y(group, slot):
        for c in y_relay(group, slot):
            c.start()

    def pass_x(group, slot):
        for c in y_relay(group, slot):
            c.wait_recv()
        for c in x_copies(group + 1, slot, 1):
            c.start()

    def finish_x(group, slot):
        for c in x_copies(group + 1, slot, 1):
            c.wait_recv()
        combine(slot, 1)

    moved_early = shift_ref[0] == 0

    @pl.when(has_lower)
    def _():
        for f in fields:
            z_up(f, 0).wait_recv()
        start_y(0, below)

    @pl.when(has_upper)
    def _():
        for f in fields:
            z_down(f, 0).wait_recv()

    start_y(1, above)
    for c in own_x:
        c.wait_recv()
    combine(FIRST, planes)
    step0(1)
    step0(2)

    @pl.when(has_lower)
    def _():
        pass_x(0, below)

    pass_x(1, above)

    @pl.when(has_upper)
    def _():
        for f in fields:
            z_down(f, 1).wait_recv()
        start_y(2, above + 1)
        for f in fields:
            for c in z_edge(f):
                c.wait_recv()
        for side in range(2):
            y_edge(side).start()

    @pl.when(has_lower)
    def _():
        finish_x(0, below)

    finish_x(1, above)
    step0(0)
    step0(3)
    put1(0, pick(jnp.logical_and(at_bottom, moved_early), t1(1), t1(0)))
    step1(1)
    step1(2)

    @pl.when(has_lower)
    def _():
        for f in fields:
            z_up(f, 1).wait_recv()

    step0(-1)
    put1(-1, pick(at_bottom, t1(0), t1(-1)))
    step1(0)
    put2(0, pick(at_bottom, t2(1), t2(0)))
    step2(1)

    @pl.when(has_upper)
    def _():
        pass_x(2, above + 1)
        for f in fields:
            z_down(f, 2).wait_recv()
        for side in range(2):
            y_edge(side).wait_recv()
        for c in x_copies(4, above + 2, 1):
            c.start()
        finish_x(2, above + 1)

    step0(4)
    put1(4, pick(at_top, pick(moved_early, t0(4), t1(3)), t1(4)))
    step1(3)
    step2(2)

    @pl.when(has_upper)
    def _():
        finish_x(3, above + 2)

    step0(5)
    put1(5, pick(at_top, t1(4), t1(5)))
    step1(4)
    put2(4, pick(jnp.logical_and(at_top, jnp.logical_not(moved_early)), t0(4), t2(4)))
    step2(3)

    for r in range(rows // TILE):
        @pl.when(has_upper)
        def _():
            for f in fields:
                z_last(f, r).wait_recv()

        v1 = advance_tile(start, FIRST + 6, r, tile(start, FIRST + 5, r), tile(start, FIRST + 7, r), 6, 0)
        v2 = advance_tile(one, 6, r, tile(one, 5, r), v1, 5, 1)
        v2 = pick(at_top, tile(two, 4, r), v2)
        a, b = advance_tile(two, 4, r, tile(two, 3, r), v2, 4, 2)
        phi_out[3, pl.ds(TILE * r, TILE)] = a[:, :lanes]
        sol_out[3, pl.ds(TILE * r, TILE)] = b[:, :lanes]

    for c in own_y + list(own_x):
        c.wait_send()
    for c in y_relay(1, above) + x_copies(2, above, 1):
        c.wait_send()

    @pl.when(has_lower)
    def _():
        for f in fields:
            for plane in range(planes - 1):
                z_down(f, plane).wait_send()
            for c in z_edge(f):
                c.wait_send()
            for r in range(rows // TILE):
                z_last(f, r).wait_send()
        for c in y_relay(0, below) + x_copies(1, below, 1):
            c.wait_send()

    @pl.when(has_upper)
    def _():
        for k in range(2):
            for f in fields:
                z_up(f, k).wait_send()
        for side in range(2):
            y_edge(side).wait_send()
        for c in y_relay(2, above + 1) + x_copies(3, above + 1, 1) + x_copies(4, above + 2, 1):
            c.wait_send()


def write_out(phi_ref, sol_ref, phi_out, sol_out, sem):
    copies = [pltpu.make_async_copy(phi_ref, phi_out, sem.at[0]), pltpu.make_async_copy(sol_ref, sol_out, sem.at[1])]
    for copy in copies:
        copy.start()
    for copy in copies:
        copy.wait()


def shards(phase_field, solute_field, shift_step, inflow_seed):
    planes, rows, lanes = phase_field.shape
    tall, wide = rows + 2 * EDGE, lanes + COL
    field = jax.ShapeDtypeStruct(phase_field.shape, jnp.float32)
    dma = pltpu.SemaphoreType.DMA
    vmem, hbm = pl.BlockSpec(memory_space=pltpu.VMEM), pl.BlockSpec(memory_space=pl.ANY)
    slots = 2 * planes + 2
    on_chip = pltpu.VMEM(phase_field.shape, jnp.float32)
    results = pl.pallas_call(
        functools.partial(kernel, (planes, rows, lanes)),
        out_shape=(on_chip, on_chip),
        in_specs=[pl.BlockSpec(memory_space=pltpu.SMEM), hbm, hbm, hbm],
        out_specs=(vmem, vmem),
        scratch_shapes=[
            pltpu.VMEM((2, slots, tall, wide), jnp.float32),
            pltpu.VMEM((2, slots, tall, COL), jnp.float32),
            pltpu.VMEM((2, slots, tall, COL), jnp.float32),
            pltpu.VMEM((2, planes + 4, tall, wide), jnp.float32),
            pltpu.VMEM((2, planes + 2, tall, wide), jnp.float32),
            pltpu.VMEM((2, 2, TILE, lanes), jnp.float32),
            pltpu.VMEM((rows, lanes), jnp.int32),
            dma((3,)), dma((6,)), dma((6,)), dma((rows // 4,)), dma((rows // 4,)), dma((2 * (planes + 2),)), dma((2 * (planes + 2),)),
            dma((4,)), dma((4,)), dma((6,)), dma((6,)), dma((10,)), dma((10,)),
        ],
        compiler_params=pltpu.CompilerParams(collective_id=0, has_side_effects=True),
    )(shift_step, inflow_seed, phase_field, solute_field)
    return pl.pallas_call(
        write_out,
        out_shape=(field, field),
        in_specs=[vmem, vmem],
        out_specs=(hbm, hbm),
        scratch_shapes=[dma((2,))],
    )(*(pltpu.with_memory_space_constraint(x, pltpu.VMEM) for x in results))


def solution(mesh):
    return jax.shard_map(
        shards,
        mesh=mesh,
        in_specs=(
            P(("groups", "grow"), "cross", "side"),
            P(("groups", "grow"), "cross", "side"),
            P("groups"),
            P(("groups", "cross"), "side"),
        ),
        out_specs=(P(("groups", "grow"), "cross", "side"), P(("groups", "grow"), "cross", "side")),
        check_vma=False,
    )
```

```python
import functools

import jax
import jax.numpy as jnp
from jax import lax
from jax.experimental import pallas as pl
from jax.experimental.pallas import tpu as pltpu
from jax.sharding import PartitionSpec as P

partition = 0.15
coupling = 2.0
diffusion = 2.0
spacing_sq = 0.64
time_step = 0.025
gradient_scale = 1.2
drift_rate = 0.01
seed_levels = 1024.0

MESH = pl.DeviceIdType.MESH
EDGE = 4
TILE = 8
COL = 128
FIRST = 2


def kernel(sizes, shift_ref, seed_ref, phi_in, sol_in, phi_out, sol_out,
           start, col_next, col_prev, one, two, edges, seed_vmem,
           local_sem, edge_send, edge_recv, last_send, last_recv, z_send, z_recv, y0_send, y0_recv, y_send, y_recv, x_send, x_recv):
    planes, rows, lanes = sizes
    inputs = (phi_in, sol_in)
    gi = lax.axis_index("grow")
    g_last = lax.axis_size("grow") - 1
    ci, c_n = lax.axis_index("cross"), lax.axis_size("cross")
    si, s_n = lax.axis_index("side"), lax.axis_size("side")
    c_next, c_prev = lax.rem(ci + 1, c_n), lax.rem(ci + c_n - 1, c_n)
    s_next, s_prev = lax.rem(si + 1, s_n), lax.rem(si + s_n - 1, s_n)
    wide, tall = lanes + COL, rows + 2 * EDGE
    at_bottom, at_top = gi == 0, gi == g_last
    inside = (pl.ds(0, rows), pl.ds(0, lanes))

    def remote(src, dst, send, recv, **where):
        return pltpu.make_async_remote_copy(src_ref=src, dst_ref=dst, send_sem=send, recv_sem=recv,
                                            device_id=where, device_id_type=MESH)

    pieces = ((0, TILE), (rows - TILE, TILE), (TILE, rows - 2 * TILE))

    def z_piece(field, plane, slot, which, order, near):
        first, count = pieces[which]
        part = pl.ds(first, count)
        n = len(pieces) * (2 * order + field) + which
        return remote(inputs[field].at[plane, part, :], start.at[field, slot, part, pl.ds(0, lanes)],
                      z_send.at[n], z_recv.at[n], grow=near)

    def z_down(field, plane, which):
        return z_piece(field, plane, FIRST + planes + plane, which, plane, gi - 1)

    def z_up(field, k, which):
        return z_piece(field, planes - 1 - k, FIRST - 1 - k, which, planes + k, gi + 1)

    def y_pair(src_of, dst_of, count, send, recv, first, **where):
        low = remote(src_of(pl.ds(0, count)), dst_of(pl.ds(rows, count)),
                     send.at[first], recv.at[first], cross=c_prev, **where)
        high = remote(src_of(pl.ds(rows - count, count)), dst_of(pl.ds(tall - count, count)),
                      send.at[first + 1], recv.at[first + 1], cross=c_next, **where)
        return low, high

    def y_own(field):
        return y_pair(lambda r: inputs[field].at[:, r, :],
                      lambda r: start.at[field, pl.ds(FIRST, planes), r, pl.ds(0, lanes)],
                      3, y0_send, y0_recv, 2 * field)

    def y_relay(group, slot):
        view = lambda r: start.at[:, slot, r, pl.ds(0, lanes)]
        return y_pair(view, view, (1, 3, 2)[group], y_send, y_recv, 2 * group)

    def z_edge(field):
        plane = inputs[field].at[planes - 2]
        return [remote(plane.at[pl.ds(row, 1), :], edges.at[field, side, pl.ds(0, 1), :],
                       edge_send.at[2 * field + side], edge_recv.at[2 * field + side], grow=gi - 1)
                for side, row in ((0, 0), (1, rows - 1))]

    def y_edge(side):
        row, where = ((rows, c_prev), (tall - 1, c_next))[side]
        return remote(edges.at[:, side, pl.ds(0, 1), :],
                      start.at[:, FIRST + 2 * planes - 2, pl.ds(row, 1), pl.ds(0, lanes)],
                      edge_send.at[4 + side], edge_recv.at[4 + side], cross=where)

    def z_last(field, r):
        part = pl.ds(TILE * r, TILE)
        return remote(inputs[field].at[planes - 1, part, :],
                      start.at[field, FIRST + 2 * planes - 1, part, pl.ds(0, lanes)],
                      last_send.at[2 * r + field], last_recv.at[2 * r + field], grow=gi - 1)

    def x_copies(group, slot, count):
        own = pl.ds(slot, count)
        low = remote(start.at[:, own, :, pl.ds(0, COL)], col_next.at[:, own],
                     x_send.at[2 * group], x_recv.at[2 * group], side=s_prev)
        high = remote(start.at[:, own, :, pl.ds(lanes - COL, COL)], col_prev.at[:, own],
                      x_send.at[2 * group + 1], x_recv.at[2 * group + 1], side=s_next)
        return low, high

    def combine(slot, count):
        near = lax.broadcasted_iota(jnp.int32, (rows + 2 * EDGE, COL), 1) < COL // 2
        for s in range(slot, slot + count):
            for f in range(2):
                start[f, s, :, pl.ds(lanes, COL)] = jnp.where(near, col_next[f, s], col_prev[f, s])

    grid_rows = planes * lax.axis_size("grow")

    def flux(w, u, wn, un):
        return (w + wn) * (un - u)

    def hole(phases):
        return 1.0 - jnp.clip(phases, -1.0, 1.0)

    def update(p, u, w, total, flow, plane, step):
        height = (gi * planes + plane).astype(jnp.float32)
        temper = gradient_scale * ((height + 0.5) / grid_rows - 0.5) - drift_rate * step
        laplace = (total - 6.0 * p) * (1.0 / spacing_sq)
        room = 1.0 - p * p
        driving = laplace + p * room - coupling * (room * room) * (u + temper)
        slowing = 1.0 - (1.0 - partition) * temper
        change = driving * (time_step / jnp.full((1, wide), slowing, jnp.float32))
        gain = flow * (0.5 * time_step * diffusion / spacing_sq) + (1.0 + (1.0 - partition) * u) * change
        weight = 2.0 * partition + (1.0 - partition) * w
        return p + change, u + gain / weight

    def along(p, u, w, axis, size):
        pn, un = pltpu.roll(p, size - 1, axis), pltpu.roll(u, size - 1, axis)
        f = flux(w, u, hole(pn), un)
        return pn + pltpu.roll(p, 1, axis), f - pltpu.roll(f, 1, axis)

    def advance(center, lower, upper, plane, step):
        p, u = center
        w = hole(p)
        total = lower[0] + upper[0]
        flow = flux(w, u, hole(lower[0]), lower[1]) + flux(w, u, hole(upper[0]), upper[1])
        for axis, size in ((0, tall), (1, wide)):
            t, f = along(p, u, w, axis, size)
            total, flow = total + t, flow + f
        return update(p, u, w, total, flow, plane, step)

    def tile(buf, slot, r):
        part = pl.ds(TILE * r, TILE)
        return buf[0, slot, part, :], buf[1, slot, part, :]

    def advance_tile(buf, slot, r, lower, upper, plane, step):
        count = tall // TILE
        p, u = tile(buf, slot, r)
        before, after = tile(buf, slot, (r - 1) % count), tile(buf, slot, (r + 1) % count)
        w = hole(p)
        total, flow = along(p, u, w, 1, wide)
        pb, ub = (pltpu.roll(jnp.concatenate([a, b]), 1, 0)[TILE:] for a, b in zip(before, (p, u)))
        pa, ua = (pltpu.roll(jnp.concatenate([b, a]), 2 * TILE - 1, 0)[:TILE] for a, b in zip(after, (p, u)))
        for pn, un in ((pb, ub), (pa, ua), lower, upper):
            total, flow = total + pn, flow + flux(w, u, hole(pn), un)
        return update(p, u, w, total, flow, plane, step)

    def pick(cond, a, b):
        return tuple(jnp.where(cond, x, y) for x, y in zip(a, b))

    def t0(k):
        return start[0, FIRST + k], start[1, FIRST + k]

    def t1(k):
        return one[0, 1 + k], one[1, 1 + k]

    def t2(k):
        return two[0, k], two[1, k]

    def put1(k, v):
        one[0, 1 + k], one[1, 1 + k] = v

    def put2(k, v):
        two[0, k], two[1, k] = v

    last = planes

    def step0(k):
        lower, upper = t0(k - 1), t0(k + 1)
        if k == 0:
            lower = pick(at_bottom, t0(0), lower)
        if k == last - 1:
            upper = pick(at_top, t0(k), upper)
        put1(k, advance(t0(k), lower, upper, k, 0))

    def step1(k):
        put2(k, advance(t1(k), t1(k - 1), t1(k + 1), k, 1))

    def step2(k):
        a, b = advance(t2(k), t2(k - 1), t2(k + 1), k, 2)
        phi_out[k - 1] = a[:rows, :lanes]
        sol_out[k - 1] = b[:rows, :lanes]

    own_copies = [pltpu.make_async_copy(inputs[f], start.at[(f, pl.ds(FIRST, planes)) + inside], local_sem.at[f])
                  for f in range(2)]
    for copy in own_copies:
        copy.start()

    @pl.when(at_top)
    def _():
        seeds = pltpu.make_async_copy(seed_ref, seed_vmem, local_sem.at[2])
        seeds.start()
        seeds.wait()
        start[(0, FIRST + planes) + inside] = jnp.full((rows, lanes), -1.0, jnp.float32)
        start[(1, FIRST + planes) + inside] = seed_vmem[...].astype(jnp.float32) / seed_levels - 1.0

    barrier = pltpu.get_barrier_semaphore()
    for where in (dict(cross=c_next), dict(cross=c_prev), dict(side=s_next), dict(side=s_prev)):
        pl.semaphore_signal(barrier, inc=1, device_id=where, device_id_type=MESH)

    for edge, near in ((at_bottom, gi - 1), (at_top, gi + 1)):
        @pl.when(jnp.logical_not(edge))
        def _():
            pl.semaphore_signal(barrier, inc=1, device_id=dict(grow=near), device_id_type=MESH)

    ends = at_bottom.astype(jnp.int32) + at_top.astype(jnp.int32)
    pl.semaphore_wait(barrier, 6 - ends)

    fields = range(2)
    has_lower, has_upper = jnp.logical_not(at_bottom), jnp.logical_not(at_top)

    @pl.when(has_lower)
    def _():
        for plane in range(planes - 1):
            for which in range(3):
                for f in fields:
                    z_down(f, plane, which).start()
            if plane == 0:
                for f in fields:
                    for c in z_edge(f):
                        c.start()
        for r in range(rows // TILE):
            for f in fields:
                z_last(f, r).start()

    @pl.when(has_upper)
    def _():
        for k in range(2):
            for which in range(3):
                for f in fields:
                    z_up(f, k, which).start()

    own_y = [c for f in fields for c in y_own(f)]
    for c in own_y:
        c.start()
    for copy in own_copies:
        copy.wait()
    for c in own_y:
        c.wait_recv()
    own_x = x_copies(0, FIRST, planes)
    for c in own_x:
        c.start()

    below, above = FIRST - 1, FIRST + planes

    def arrived(copy_of, k, parts):
        for which in parts:
            for f in fields:
                copy_of(f, k, which).wait_recv()

    edge_parts, middle, whole = (0, 1), (2,), (0, 1, 2)

    def start_y(group, slot):
        for c in y_relay(group, slot):
            c.start()

    def pass_x(group, slot):
        for c in y_relay(group, slot):
            c.wait_recv()
        for c in x_copies(group + 1, slot, 1):
            c.start()

    def finish_x(group, slot):
        for c in x_copies(group + 1, slot, 1):
            c.wait_recv()
        combine(slot, 1)

    moved_early = shift_ref[0] == 0

    @pl.when(has_lower)
    def _():
        arrived(z_up, 0, edge_parts)
        start_y(0, below)

    @pl.when(has_upper)
    def _():
        arrived(z_down, 0, edge_parts)

    start_y(1, above)
    for c in own_x:
        c.wait_recv()
    combine(FIRST, planes)
    step0(1)
    step0(2)

    @pl.when(has_lower)
    def _():
        arrived(z_up, 0, middle)
        pass_x(0, below)

    @pl.when(has_upper)
    def _():
        arrived(z_down, 0, middle)

    pass_x(1, above)

    @pl.when(has_upper)
    def _():
        arrived(z_down, 1, edge_parts)
        start_y(2, above + 1)
        for f in fields:
            for c in z_edge(f):
                c.wait_recv()
        for side in range(2):
            y_edge(side).start()

    @pl.when(has_lower)
    def _():
        finish_x(0, below)

    finish_x(1, above)
    step0(0)
    step0(3)
    put1(0, pick(jnp.logical_and(at_bottom, moved_early), t1(1), t1(0)))
    step1(1)
    step1(2)

    @pl.when(has_lower)
    def _():
        arrived(z_up, 1, whole)

    step0(-1)
    put1(-1, pick(at_bottom, t1(0), t1(-1)))
    step1(0)
    put2(0, pick(at_bottom, t2(1), t2(0)))
    step2(1)

    @pl.when(has_upper)
    def _():
        arrived(z_down, 1, middle)
        pass_x(2, above + 1)
        arrived(z_down, 2, whole)
        for side in range(2):
            y_edge(side).wait_recv()
        for c in x_copies(4, above + 2, 1):
            c.start()
        finish_x(2, above + 1)

    step0(4)
    put1(4, pick(at_top, pick(moved_early, t0(4), t1(3)), t1(4)))
    step1(3)
    step2(2)

    @pl.when(has_upper)
    def _():
        finish_x(3, above + 2)

    step0(5)
    put1(5, pick(at_top, t1(4), t1(5)))
    step1(4)
    put2(4, pick(jnp.logical_and(at_top, jnp.logical_not(moved_early)), t0(4), t2(4)))
    step2(3)

    for r in range(rows // TILE):
        @pl.when(has_upper)
        def _():
            for f in fields:
                z_last(f, r).wait_recv()

        v1 = advance_tile(start, FIRST + 6, r, tile(start, FIRST + 5, r), tile(start, FIRST + 7, r), 6, 0)
        v2 = advance_tile(one, 6, r, tile(one, 5, r), v1, 5, 1)
        v2 = pick(at_top, tile(two, 4, r), v2)
        a, b = advance_tile(two, 4, r, tile(two, 3, r), v2, 4, 2)
        phi_out[3, pl.ds(TILE * r, TILE)] = a[:, :lanes]
        sol_out[3, pl.ds(TILE * r, TILE)] = b[:, :lanes]

    for c in own_y + list(own_x):
        c.wait_send()
    for c in y_relay(1, above) + x_copies(2, above, 1):
        c.wait_send()

    @pl.when(has_lower)
    def _():
        for f in fields:
            for plane in range(planes - 1):
                for which in range(3):
                    z_down(f, plane, which).wait_send()
            for c in z_edge(f):
                c.wait_send()
            for r in range(rows // TILE):
                z_last(f, r).wait_send()
        for c in y_relay(0, below) + x_copies(1, below, 1):
            c.wait_send()

    @pl.when(has_upper)
    def _():
        for k in range(2):
            for f in fields:
                for which in range(3):
                    z_up(f, k, which).wait_send()
        for side in range(2):
            y_edge(side).wait_send()
        for c in y_relay(2, above + 1) + x_copies(3, above + 1, 1) + x_copies(4, above + 2, 1):
            c.wait_send()


def write_out(phi_ref, sol_ref, phi_out, sol_out, sem):
    copies = [pltpu.make_async_copy(phi_ref, phi_out, sem.at[0]), pltpu.make_async_copy(sol_ref, sol_out, sem.at[1])]
    for copy in copies:
        copy.start()
    for copy in copies:
        copy.wait()


def shards(phase_field, solute_field, shift_step, inflow_seed):
    planes, rows, lanes = phase_field.shape
    tall, wide = rows + 2 * EDGE, lanes + COL
    field = jax.ShapeDtypeStruct(phase_field.shape, jnp.float32)
    dma = pltpu.SemaphoreType.DMA
    vmem, hbm = pl.BlockSpec(memory_space=pltpu.VMEM), pl.BlockSpec(memory_space=pl.ANY)
    slots = 2 * planes + 2
    on_chip = pltpu.VMEM(phase_field.shape, jnp.float32)
    results = pl.pallas_call(
        functools.partial(kernel, (planes, rows, lanes)),
        out_shape=(on_chip, on_chip),
        in_specs=[pl.BlockSpec(memory_space=pltpu.SMEM), hbm, hbm, hbm],
        out_specs=(vmem, vmem),
        scratch_shapes=[
            pltpu.VMEM((2, slots, tall, wide), jnp.float32),
            pltpu.VMEM((2, slots, tall, COL), jnp.float32),
            pltpu.VMEM((2, slots, tall, COL), jnp.float32),
            pltpu.VMEM((2, planes + 4, tall, wide), jnp.float32),
            pltpu.VMEM((2, planes + 2, tall, wide), jnp.float32),
            pltpu.VMEM((2, 2, TILE, lanes), jnp.float32),
            pltpu.VMEM((rows, lanes), jnp.int32),
            dma((3,)), dma((6,)), dma((6,)), dma((rows // 4,)), dma((rows // 4,)), dma((6 * (planes + 2),)), dma((6 * (planes + 2),)),
            dma((4,)), dma((4,)), dma((6,)), dma((6,)), dma((10,)), dma((10,)),
        ],
        compiler_params=pltpu.CompilerParams(collective_id=0, has_side_effects=True),
    )(shift_step, inflow_seed, phase_field, solute_field)
    return pl.pallas_call(
        write_out,
        out_shape=(field, field),
        in_specs=[vmem, vmem],
        out_specs=(hbm, hbm),
        scratch_shapes=[dma((2,))],
    )(*(pltpu.with_memory_space_constraint(x, pltpu.VMEM) for x in results))


def solution(mesh):
    return jax.shard_map(
        shards,
        mesh=mesh,
        in_specs=(
            P(("groups", "grow"), "cross", "side"),
            P(("groups", "grow"), "cross", "side"),
            P("groups"),
            P(("groups", "cross"), "side"),
        ),
        out_specs=(P(("groups", "grow"), "cross", "side"), P(("groups", "grow"), "cross", "side")),
        check_vma=False,
    )
```

```python
import functools

import jax
import jax.numpy as jnp
from jax import lax
from jax.experimental import pallas as pl
from jax.experimental.pallas import tpu as pltpu
from jax.sharding import PartitionSpec as P

partition = 0.15
coupling = 2.0
diffusion = 2.0
spacing_sq = 0.64
time_step = 0.025
gradient_scale = 1.2
drift_rate = 0.01
seed_levels = 1024.0

MESH = pl.DeviceIdType.MESH
EDGE = 4
TILE = 8
COL = 128
FIRST = 2


def kernel(sizes, shift_ref, seed_ref, phi_in, sol_in, phi_out, sol_out,
           start, col_next, col_prev, one, two, edges, seed_vmem,
           local_sem, edge_send, edge_recv, last_send, last_recv, z_send, z_recv, y0_send, y0_recv, y_send, y_recv, x_send, x_recv):
    planes, rows, lanes = sizes
    inputs = (phi_in, sol_in)
    gi = lax.axis_index("grow")
    g_last = lax.axis_size("grow") - 1
    ci, c_n = lax.axis_index("cross"), lax.axis_size("cross")
    si, s_n = lax.axis_index("side"), lax.axis_size("side")
    c_next, c_prev = lax.rem(ci + 1, c_n), lax.rem(ci + c_n - 1, c_n)
    s_next, s_prev = lax.rem(si + 1, s_n), lax.rem(si + s_n - 1, s_n)
    wide, tall = lanes + COL, rows + 2 * EDGE
    at_bottom, at_top = gi == 0, gi == g_last
    inside = (pl.ds(0, rows), pl.ds(0, lanes))

    def remote(src, dst, send, recv, **where):
        return pltpu.make_async_remote_copy(src_ref=src, dst_ref=dst, send_sem=send, recv_sem=recv,
                                            device_id=where, device_id_type=MESH)

    pieces = ((0, TILE), (rows - TILE, TILE), (TILE, rows - 2 * TILE))

    def z_piece(field, plane, slot, which, order, near):
        first, count = pieces[which]
        part = pl.ds(first, count)
        n = len(pieces) * (2 * order + field) + which
        return remote(inputs[field].at[plane, part, :], start.at[field, slot, part, pl.ds(0, lanes)],
                      z_send.at[n], z_recv.at[n], grow=near)

    def z_down(field, plane, which):
        return z_piece(field, plane, FIRST + planes + plane, which, plane, gi - 1)

    def z_up(field, k, which):
        return z_piece(field, planes - 1 - k, FIRST - 1 - k, which, planes + k, gi + 1)

    def y_pair(src_of, dst_of, count, send, recv, first, **where):
        low = remote(src_of(pl.ds(0, count)), dst_of(pl.ds(rows, count)),
                     send.at[first], recv.at[first], cross=c_prev, **where)
        high = remote(src_of(pl.ds(rows - count, count)), dst_of(pl.ds(tall - count, count)),
                      send.at[first + 1], recv.at[first + 1], cross=c_next, **where)
        return low, high

    def y_own(field):
        return y_pair(lambda r: inputs[field].at[:, r, :],
                      lambda r: start.at[field, pl.ds(FIRST, planes), r, pl.ds(0, lanes)],
                      3, y0_send, y0_recv, 2 * field)

    def y_relay(group, slot):
        view = lambda r: start.at[:, slot, r, pl.ds(0, lanes)]
        return y_pair(view, view, (1, 3, 2)[group], y_send, y_recv, 2 * group)

    def z_edge(field):
        plane = inputs[field].at[planes - 2]
        return [remote(plane.at[pl.ds(row, 1), :], edges.at[field, side, pl.ds(0, 1), :],
                       edge_send.at[2 * field + side], edge_recv.at[2 * field + side], grow=gi - 1)
                for side, row in ((0, 0), (1, rows - 1))]

    def y_edge(side):
        row, where = ((rows, c_prev), (tall - 1, c_next))[side]
        return remote(edges.at[:, side, pl.ds(0, 1), :],
                      start.at[:, FIRST + 2 * planes - 2, pl.ds(row, 1), pl.ds(0, lanes)],
                      edge_send.at[4 + side], edge_recv.at[4 + side], cross=where)

    def z_last(field, r):
        part = pl.ds(TILE * r, TILE)
        return remote(inputs[field].at[planes - 1, part, :],
                      start.at[field, FIRST + 2 * planes - 1, part, pl.ds(0, lanes)],
                      last_send.at[2 * r + field], last_recv.at[2 * r + field], grow=gi - 1)

    def x_copies(group, slot, count):
        own = pl.ds(slot, count)
        low = remote(start.at[:, own, :, pl.ds(0, COL)], col_next.at[:, own],
                     x_send.at[2 * group], x_recv.at[2 * group], side=s_prev)
        high = remote(start.at[:, own, :, pl.ds(lanes - COL, COL)], col_prev.at[:, own],
                      x_send.at[2 * group + 1], x_recv.at[2 * group + 1], side=s_next)
        return low, high

    def combine(slot, count):
        near = lax.broadcasted_iota(jnp.int32, (rows + 2 * EDGE, COL), 1) < COL // 2
        for s in range(slot, slot + count):
            for f in range(2):
                start[f, s, :, pl.ds(lanes, COL)] = jnp.where(near, col_next[f, s], col_prev[f, s])

    grid_rows = planes * lax.axis_size("grow")

    def flux(w, u, wn, un):
        return (w + wn) * (un - u)

    def hole(phases):
        return 1.0 - jnp.clip(phases, -1.0, 1.0)

    def update(p, u, w, total, flow, plane, step):
        height = (gi * planes + plane).astype(jnp.float32)
        temper = gradient_scale * ((height + 0.5) / grid_rows - 0.5) - drift_rate * step
        laplace = (total - 6.0 * p) * (1.0 / spacing_sq)
        room = 1.0 - p * p
        driving = laplace + p * room - coupling * (room * room) * (u + temper)
        slowing = 1.0 - (1.0 - partition) * temper
        change = driving * (time_step / jnp.full((1, wide), slowing, jnp.float32))
        gain = flow * (0.5 * time_step * diffusion / spacing_sq) + (1.0 + (1.0 - partition) * u) * change
        weight = 2.0 * partition + (1.0 - partition) * w
        return p + change, u + gain / weight

    def along(p, u, w, axis, size):
        pn, un = pltpu.roll(p, size - 1, axis), pltpu.roll(u, size - 1, axis)
        f = flux(w, u, hole(pn), un)
        return pn + pltpu.roll(p, 1, axis), f - pltpu.roll(f, 1, axis)

    def advance(center, lower, upper, plane, step):
        p, u = center
        w = hole(p)
        total = lower[0] + upper[0]
        flow = flux(w, u, hole(lower[0]), lower[1]) + flux(w, u, hole(upper[0]), upper[1])
        for axis, size in ((0, tall), (1, wide)):
            t, f = along(p, u, w, axis, size)
            total, flow = total + t, flow + f
        return update(p, u, w, total, flow, plane, step)

    def tile(buf, slot, r):
        part = pl.ds(TILE * r, TILE)
        return buf[0, slot, part, :], buf[1, slot, part, :]

    def advance_tile(buf, slot, r, lower, upper, plane, step):
        count = tall // TILE
        p, u = tile(buf, slot, r)
        before, after = tile(buf, slot, (r - 1) % count), tile(buf, slot, (r + 1) % count)
        w = hole(p)
        total, flow = along(p, u, w, 1, wide)
        pb, ub = (pltpu.roll(jnp.concatenate([a, b]), 1, 0)[TILE:] for a, b in zip(before, (p, u)))
        pa, ua = (pltpu.roll(jnp.concatenate([b, a]), 2 * TILE - 1, 0)[:TILE] for a, b in zip(after, (p, u)))
        for pn, un in ((pb, ub), (pa, ua), lower, upper):
            total, flow = total + pn, flow + flux(w, u, hole(pn), un)
        return update(p, u, w, total, flow, plane, step)

    def pick(cond, a, b):
        return tuple(jnp.where(cond, x, y) for x, y in zip(a, b))

    def t0(k):
        return start[0, FIRST + k], start[1, FIRST + k]

    def t1(k):
        return one[0, 1 + k], one[1, 1 + k]

    def t2(k):
        return two[0, k], two[1, k]

    def put1(k, v):
        one[0, 1 + k], one[1, 1 + k] = v

    def put2(k, v):
        two[0, k], two[1, k] = v

    last = planes

    def step0(k):
        lower, upper = t0(k - 1), t0(k + 1)
        if k == 0:
            lower = pick(at_bottom, t0(0), lower)
        if k == last - 1:
            upper = pick(at_top, t0(k), upper)
        put1(k, advance(t0(k), lower, upper, k, 0))

    def step1(k):
        put2(k, advance(t1(k), t1(k - 1), t1(k + 1), k, 1))

    def step2(k):
        a, b = advance(t2(k), t2(k - 1), t2(k + 1), k, 2)
        phi_out[k - 1] = a[:rows, :lanes]
        sol_out[k - 1] = b[:rows, :lanes]

    own_copies = [pltpu.make_async_copy(inputs[f], start.at[(f, pl.ds(FIRST, planes)) + inside], local_sem.at[f])
                  for f in range(2)]
    for copy in own_copies:
        copy.start()

    @pl.when(at_top)
    def _():
        seeds = pltpu.make_async_copy(seed_ref, seed_vmem, local_sem.at[2])
        seeds.start()
        seeds.wait()
        start[(0, FIRST + planes) + inside] = jnp.full((rows, lanes), -1.0, jnp.float32)
        start[(1, FIRST + planes) + inside] = seed_vmem[...].astype(jnp.float32) / seed_levels - 1.0

    barrier = pltpu.get_barrier_semaphore()
    for where in (dict(cross=c_next), dict(cross=c_prev), dict(side=s_next), dict(side=s_prev)):
        pl.semaphore_signal(barrier, inc=1, device_id=where, device_id_type=MESH)

    for edge, near in ((at_bottom, gi - 1), (at_top, gi + 1)):
        @pl.when(jnp.logical_not(edge))
        def _():
            pl.semaphore_signal(barrier, inc=1, device_id=dict(grow=near), device_id_type=MESH)

    ends = at_bottom.astype(jnp.int32) + at_top.astype(jnp.int32)
    pl.semaphore_wait(barrier, 6 - ends)

    fields = range(2)
    has_lower, has_upper = jnp.logical_not(at_bottom), jnp.logical_not(at_top)

    def start_down(plane):
        for which in range(3):
            for f in fields:
                z_down(f, plane, which).start()

    @pl.when(has_lower)
    def _():
        start_down(0)
        for f in fields:
            for c in z_edge(f):
                c.start()

    own_y = [c for f in fields for c in y_own(f)]
    for c in own_y:
        c.start()

    @pl.when(has_upper)
    def _():
        for k in range(2):
            for which in range(3):
                for f in fields:
                    z_up(f, k, which).start()

    @pl.when(has_lower)
    def _():
        for plane in range(1, planes - 1):
            start_down(plane)
        for r in range(rows // TILE):
            for f in fields:
                z_last(f, r).start()

    for copy in own_copies:
        copy.wait()
    for c in own_y:
        c.wait_recv()
    own_x = x_copies(0, FIRST, planes)
    for c in own_x:
        c.start()

    below, above = FIRST - 1, FIRST + planes

    def arrived(copy_of, k, parts):
        for which in parts:
            for f in fields:
                copy_of(f, k, which).wait_recv()

    edge_parts, middle, whole = (0, 1), (2,), (0, 1, 2)

    def start_y(group, slot):
        for c in y_relay(group, slot):
            c.start()

    def pass_x(group, slot):
        for c in y_relay(group, slot):
            c.wait_recv()
        for c in x_copies(group + 1, slot, 1):
            c.start()

    def finish_x(group, slot):
        for c in x_copies(group + 1, slot, 1):
            c.wait_recv()
        combine(slot, 1)

    moved_early = shift_ref[0] == 0

    @pl.when(has_lower)
    def _():
        arrived(z_up, 0, edge_parts)
        start_y(0, below)

    @pl.when(has_upper)
    def _():
        arrived(z_down, 0, edge_parts)

    start_y(1, above)
    for c in own_x:
        c.wait_recv()
    combine(FIRST, planes)
    step0(1)
    step0(2)

    @pl.when(has_lower)
    def _():
        arrived(z_up, 0, middle)
        pass_x(0, below)

    @pl.when(has_upper)
    def _():
        arrived(z_down, 0, middle)

    pass_x(1, above)

    @pl.when(has_upper)
    def _():
        arrived(z_down, 1, edge_parts)
        start_y(2, above + 1)
        for f in fields:
            for c in z_edge(f):
                c.wait_recv()
        for side in range(2):
            y_edge(side).start()

    @pl.when(has_lower)
    def _():
        finish_x(0, below)

    finish_x(1, above)
    step0(0)
    step0(3)
    put1(0, pick(jnp.logical_and(at_bottom, moved_early), t1(1), t1(0)))
    step1(1)
    step1(2)

    @pl.when(has_lower)
    def _():
        arrived(z_up, 1, whole)

    step0(-1)
    put1(-1, pick(at_bottom, t1(0), t1(-1)))
    step1(0)
    put2(0, pick(at_bottom, t2(1), t2(0)))
    step2(1)

    @pl.when(has_upper)
    def _():
        arrived(z_down, 1, middle)
        pass_x(2, above + 1)
        arrived(z_down, 2, whole)
        for side in range(2):
            y_edge(side).wait_recv()
        for c in x_copies(4, above + 2, 1):
            c.start()
        finish_x(2, above + 1)

    step0(4)
    put1(4, pick(at_top, pick(moved_early, t0(4), t1(3)), t1(4)))
    step1(3)
    step2(2)

    @pl.when(has_upper)
    def _():
        finish_x(3, above + 2)

    step0(5)
    put1(5, pick(at_top, t1(4), t1(5)))
    step1(4)
    put2(4, pick(jnp.logical_and(at_top, jnp.logical_not(moved_early)), t0(4), t2(4)))
    step2(3)

    for r in range(rows // TILE):
        @pl.when(has_upper)
        def _():
            for f in fields:
                z_last(f, r).wait_recv()

        v1 = advance_tile(start, FIRST + 6, r, tile(start, FIRST + 5, r), tile(start, FIRST + 7, r), 6, 0)
        v2 = advance_tile(one, 6, r, tile(one, 5, r), v1, 5, 1)
        v2 = pick(at_top, tile(two, 4, r), v2)
        a, b = advance_tile(two, 4, r, tile(two, 3, r), v2, 4, 2)
        phi_out[3, pl.ds(TILE * r, TILE)] = a[:, :lanes]
        sol_out[3, pl.ds(TILE * r, TILE)] = b[:, :lanes]

    for c in own_y + list(own_x):
        c.wait_send()
    for c in y_relay(1, above) + x_copies(2, above, 1):
        c.wait_send()

    @pl.when(has_lower)
    def _():
        for f in fields:
            for plane in range(planes - 1):
                for which in range(3):
                    z_down(f, plane, which).wait_send()
            for c in z_edge(f):
                c.wait_send()
            for r in range(rows // TILE):
                z_last(f, r).wait_send()
        for c in y_relay(0, below) + x_copies(1, below, 1):
            c.wait_send()

    @pl.when(has_upper)
    def _():
        for k in range(2):
            for f in fields:
                for which in range(3):
                    z_up(f, k, which).wait_send()
        for side in range(2):
            y_edge(side).wait_send()
        for c in y_relay(2, above + 1) + x_copies(3, above + 1, 1) + x_copies(4, above + 2, 1):
            c.wait_send()


def write_out(phi_ref, sol_ref, phi_out, sol_out, sem):
    copies = [pltpu.make_async_copy(phi_ref, phi_out, sem.at[0]), pltpu.make_async_copy(sol_ref, sol_out, sem.at[1])]
    for copy in copies:
        copy.start()
    for copy in copies:
        copy.wait()


def shards(phase_field, solute_field, shift_step, inflow_seed):
    planes, rows, lanes = phase_field.shape
    tall, wide = rows + 2 * EDGE, lanes + COL
    field = jax.ShapeDtypeStruct(phase_field.shape, jnp.float32)
    dma = pltpu.SemaphoreType.DMA
    vmem, hbm = pl.BlockSpec(memory_space=pltpu.VMEM), pl.BlockSpec(memory_space=pl.ANY)
    slots = 2 * planes + 2
    on_chip = pltpu.VMEM(phase_field.shape, jnp.float32)
    results = pl.pallas_call(
        functools.partial(kernel, (planes, rows, lanes)),
        out_shape=(on_chip, on_chip),
        in_specs=[pl.BlockSpec(memory_space=pltpu.SMEM), hbm, hbm, hbm],
        out_specs=(vmem, vmem),
        scratch_shapes=[
            pltpu.VMEM((2, slots, tall, wide), jnp.float32),
            pltpu.VMEM((2, slots, tall, COL), jnp.float32),
            pltpu.VMEM((2, slots, tall, COL), jnp.float32),
            pltpu.VMEM((2, planes + 4, tall, wide), jnp.float32),
            pltpu.VMEM((2, planes + 2, tall, wide), jnp.float32),
            pltpu.VMEM((2, 2, TILE, lanes), jnp.float32),
            pltpu.VMEM((rows, lanes), jnp.int32),
            dma((3,)), dma((6,)), dma((6,)), dma((rows // 4,)), dma((rows // 4,)), dma((6 * (planes + 2),)), dma((6 * (planes + 2),)),
            dma((4,)), dma((4,)), dma((6,)), dma((6,)), dma((10,)), dma((10,)),
        ],
        compiler_params=pltpu.CompilerParams(collective_id=0, has_side_effects=True),
    )(shift_step, inflow_seed, phase_field, solute_field)
    return pl.pallas_call(
        write_out,
        out_shape=(field, field),
        in_specs=[vmem, vmem],
        out_specs=(hbm, hbm),
        scratch_shapes=[dma((2,))],
    )(*(pltpu.with_memory_space_constraint(x, pltpu.VMEM) for x in results))


def solution(mesh):
    return jax.shard_map(
        shards,
        mesh=mesh,
        in_specs=(
            P(("groups", "grow"), "cross", "side"),
            P(("groups", "grow"), "cross", "side"),
            P("groups"),
            P(("groups", "cross"), "side"),
        ),
        out_specs=(P(("groups", "grow"), "cross", "side"), P(("groups", "grow"), "cross", "side")),
        check_vma=False,
    )
```
